512 devices in a mesh: vel: 64 (over x_lo, z, core), box: 8 (over x_hi, y).
Axes of the slice: x: 4 (x_hi: 2, x_lo: 2; x = x_hi * 2 + x_lo), y: 4, z: 16, core: 2. Of those that a mesh axis runs over, the one named last changes fastest.
Arguments:
- distribution: float32 [4096, 3, 3, 3, 8, 128], P('vel', None, None, None, 'box'), may hold values from -2.5 to 2.5, as said below
- collision_rate: float32 [8, 128], P('box'), may hold values from 1 to 10
Outputs:
- advanced: float32 [4096, 3, 3, 3, 8, 128], P('vel', None, None, None, 'box')
The draws below stay inside these ranges and needn't reach their ends.
Inputs may be any that keep to these rules, and one draw needn't show every extreme that they name: `distribution`: coefficient (0,0,0) is positive for every box and velocity; every other coefficient is at most coefficient (0,0,0) of the same box and velocity in magnitude.
All inputs are finite; a program needn't handle non-finite values.
Results may differ from the reference program's by a relative error of at most 0.0003.
Values sent between devices are 32-bit elements; how exact they have to be, the bound alone decides.
No kernel may reach another device: no remote copies, remote signals or barrier semaphores. Data moves between devices by JAX's collectives and lax.ppermute only.
A program may use at most 64 MiB of HBM per device.

```python
import math
import jax
import jax.numpy as jnp
from jax import lax

VPD = 16
MODES = 3
NY = 8
NZ = 16
NX = 8
NYZ = 128


def grid_speeds():
    spacing = 8.0 / VPD
    index = jnp.arange(VPD ** 3, dtype=jnp.int32)

    def centre(number):
        return -4.0 + (number.astype(jnp.float32) + 0.5) * spacing
    return (centre(index // (VPD * VPD)), centre(index // VPD % VPD), centre(index % VPD))


def smooth_field(key):
    phases = jax.random.uniform(key, (3,), jnp.float32, 0.0, 2.0 * jnp.pi)
    along_x = jnp.sin(2.0 * jnp.pi * jnp.arange(NX, dtype=jnp.float32) / NX + phases[0])
    along_y = jnp.sin(2.0 * jnp.pi * jnp.arange(NY, dtype=jnp.float32) / NY + phases[1])
    along_z = jnp.sin(2.0 * jnp.pi * jnp.arange(NZ, dtype=jnp.float32) / NZ + phases[2])
    total = along_x[:, None, None] + along_y[None, :, None] + along_z[None, None, :]
    return (total / 3.0).reshape(NX, NY * NZ)


def draw_distribution(key, part):
    shape = (VPD ** 3, MODES, MODES, MODES, NX, NY * NZ)
    salt = 20
    density = 4.0 * 8.0 ** (0.5 * (smooth_field(jax.random.fold_in(key, salt + 1)) + 1.0))
    flow_x = smooth_field(jax.random.fold_in(key, salt + 2))
    flow_y = smooth_field(jax.random.fold_in(key, salt + 3))
    flow_z = smooth_field(jax.random.fold_in(key, salt + 4))
    temper = 4.0 ** (0.5 * (smooth_field(jax.random.fold_in(key, salt + 5)) + 1.0))
    speed_x, speed_y, speed_z = grid_speeds()
    offset_x = speed_x[:, None, None] - flow_x[None]
    offset_y = speed_y[:, None, None] - flow_y[None]
    offset_z = speed_z[:, None, None] - flow_z[None]
    spread = offset_x * offset_x + offset_y * offset_y + offset_z * offset_z
    maxwell = density[None] * (2.0 * jnp.pi * temper[None]) ** (-1.5) * jnp.exp(-spread / (2.0 * temper[None]))
    noise_key = jax.random.fold_in(key, salt + 6)
    noise = jax.random.uniform(noise_key, maxwell.shape, jnp.float32, -1.0, 1.0)
    base = maxwell * (1.0 + 0.2 * noise)
    higher = 0.2 * jax.random.truncated_normal(jax.random.fold_in(key, salt + 7), -5.0, 5.0, shape, jnp.float32)
    higher = higher * base[:, None, None, None]
    modes = jnp.arange(MODES ** 3, dtype=jnp.int32).reshape(1, MODES, MODES, MODES, 1, 1)
    return jnp.where(modes == 0, base[:, None, None, None], higher)


def block_levels(own_key, shape, split, least, high):
    gain, own = 1.0, jax.random.fold_in(own_key, 6)
    for position, blocks in split:
        steps = jnp.exp(jax.random.uniform(jax.random.fold_in(own, position), (blocks,), jnp.float32, least / len(split), high / len(split)))
        gain = gain * jnp.repeat(steps, shape[position] // blocks).reshape([-1 if axis == position else 1 for axis in range(len(shape))])
    return gain


def setup_inputs(seed: int = 0) -> dict:
    seeds = jax.random.split(jax.random.key(seed), 3)
    distribution = draw_distribution(jax.random.fold_in(seeds[2], 71), 0)
    collision_rate = jnp.clip(jnp.exp(math.log(10.0) - 2.3025851 * jax.random.uniform(seeds[1], (NX, NYZ), jnp.float32) ** block_levels(seeds[1], (NX, NYZ), ((0, 8),), -0.2, 0.2)), 1.0, 10.0)
    return {"distribution": distribution, "collision_rate": collision_rate}


SPEED_LIMIT = 4.0
TIME_STEP = 0.02
HIGHEST = lax.Precision.HIGHEST


def speeds(index):
    spacing = 2.0 * SPEED_LIMIT / VPD
    first = index // (VPD * VPD)
    second = (index // VPD) % VPD
    third = index % VPD

    def centre(number):
        return -SPEED_LIMIT + (number.astype(jnp.float32) + 0.5) * spacing

    return centre(first), centre(second), centre(third)


def moment_table(index):
    speed_x, speed_y, speed_z = speeds(index)
    weight = (2.0 * SPEED_LIMIT / VPD) ** 3
    energy = 0.5 * (speed_x * speed_x + speed_y * speed_y + speed_z * speed_z)
    return weight * jnp.stack([jnp.ones_like(speed_x), speed_x, speed_y, speed_z, energy])


def primitives(totals):
    density = totals[0]
    flow = totals[1:4] / density
    temper = (2.0 * totals[4] / density - jnp.sum(flow * flow, axis=0)) / 3.0
    return jnp.concatenate([density[None], flow, temper[None]], axis=0)


def face_traces(field, axis):
    first = jnp.take(field, 0, axis)
    second = jnp.take(field, 1, axis)
    third = jnp.take(field, 2, axis)
    return first + second + third, first - second + third


def transport(field, axis, speed, upper, lower, upper_prev, lower_next):
    positive = speed > 0
    upper_flux = jnp.where(positive, upper, lower_next)
    lower_flux = jnp.where(positive, upper_prev, lower)
    first = jnp.take(field, 0, axis)
    second = jnp.take(field, 1, axis)
    rate_zero = speed * (lower_flux - upper_flux)
    rate_one = 3.0 * speed * (2.0 * first - upper_flux - lower_flux)
    rate_two = 5.0 * speed * (2.0 * second - upper_flux + lower_flux)
    return jnp.stack([rate_zero, rate_one, rate_two], axis)


def z_previous(values):
    cells = jnp.arange(values.shape[-1], dtype=jnp.int32) % NZ
    return jnp.where(cells == 0, jnp.roll(values, 1 - NZ, -1), jnp.roll(values, 1, -1))


def z_following(values):
    cells = jnp.arange(values.shape[-1], dtype=jnp.int32) % NZ
    return jnp.where(cells == NZ - 1, jnp.roll(values, NZ - 1, -1), jnp.roll(values, -1, -1))


def block_rate(field, index, states, collision_rate, upper_prev, lower_next):
    speed_x, speed_y, speed_z = speeds(index)
    shaped = (-1, 1, 1, 1, 1)
    upper, lower = face_traces(field, 1)
    total = transport(field, 1, speed_x.reshape(shaped), upper, lower, upper_prev, lower_next)
    upper, lower = face_traces(field, 2)
    total = total + transport(field, 2, speed_y.reshape(shaped), upper, lower,
                              jnp.roll(upper, NZ, -1), jnp.roll(lower, -NZ, -1))
    upper, lower = face_traces(field, 3)
    total = total + transport(field, 3, speed_z.reshape(shaped), upper, lower,
                              z_previous(upper), z_following(lower))
    density = states[0]
    temper = states[4]
    offset_x = speed_x[:, None, None] - states[1]
    offset_y = speed_y[:, None, None] - states[2]
    offset_z = speed_z[:, None, None] - states[3]
    spread = offset_x * offset_x + offset_y * offset_y + offset_z * offset_z
    maxwell = density * (2.0 * jnp.pi * temper) ** (-1.5) * jnp.exp(-spread / (2.0 * temper))
    total = total - collision_rate * field
    return total.at[:, 0, 0, 0].add(collision_rate * maxwell)


def section_rate(field, collision_rate):
    count = field.shape[0]
    index = jnp.arange(count, dtype=jnp.int32)
    base = field[:, 0, 0, 0].reshape(count, -1)
    totals = jnp.dot(moment_table(index), base, precision=HIGHEST)
    states = primitives(totals).reshape((5,) + field.shape[4:])
    blocks = max(count // 256, 1)
    width = count // blocks

    def one_block(pair):
        piece, start = pair
        upper, lower = face_traces(piece, 1)
        local_index = start + jnp.arange(width, dtype=jnp.int32)
        return block_rate(piece, local_index, states, collision_rate,
                          jnp.roll(upper, 1, 3), jnp.roll(lower, -1, 3))

    pieces = field.reshape((blocks, width) + field.shape[1:])
    starts = jnp.arange(blocks, dtype=jnp.int32) * width
    rates = lax.map(one_block, (pieces, starts))
    return rates.reshape(field.shape)


def reference(distribution, collision_rate):
    middle = distribution + TIME_STEP * section_rate(distribution, collision_rate)
    final_rate = section_rate(middle, collision_rate)
    return 0.5 * distribution + 0.5 * (middle + TIME_STEP * final_rate)
```

```python
import math

import jax
import jax.numpy as jnp
from jax import lax
from jax.experimental import pallas as pl
from jax.experimental.pallas import tpu as pltpu
from jax.sharding import PartitionSpec as P

NZ = 16
VELS = 64
BOXES = 8
COUNT = 64
STEP = 0.02
SPACING = 0.5
FIRST = -3.75
WEIGHT = SPACING**3
ROWS = 16
TILE = 8


def mode(a, b, c):
    return 9 * a + 3 * b + c


def row_index():
    return lax.broadcasted_iota(jnp.int32, (TILE, 128), 0)


class Place:
    def __init__(self):
        self.vel = lax.axis_index("vel")
        self.box = lax.axis_index("box")
        right = self.vel >= VELS // 2
        self.sx = jnp.where(right, 1.0, -1.0)
        self.wx = (self.vel // 4).astype(jnp.float32) * SPACING + FIRST
        self.ax = self.wx * self.sx
        up = self.vel % 4 >= 2
        self.sy = jnp.where(up, 1.0, -1.0)
        self.first_y = (self.vel % 4 * 4).astype(jnp.float32) * SPACING + FIRST
        self.shift_y = jnp.where(up, NZ, 128 - NZ)
        self.upwind = jnp.where(right, (self.box + BOXES - 1) % BOXES, (self.box + 1) % BOXES)
        self.downwind = jnp.where(right, (self.box + 1) % BOXES, (self.box + BOXES - 1) % BOXES)
        self.lane = lax.broadcasted_iota(jnp.int32, (TILE, 128), 1) % NZ

    def wy(self, j):
        return self.first_y + j.astype(jnp.float32) * SPACING

    def wz(self, half):
        return row_index().astype(jnp.float32) * SPACING + (FIRST + half * TILE * SPACING)

    def from_y(self, values):
        return pltpu.roll(values, self.shift_y, 1)

    def from_z(self, values, half):
        if half:
            return jnp.where(self.lane == 0, pltpu.roll(values, 128 + 1 - NZ, 1), pltpu.roll(values, 1, 1))
        return jnp.where(self.lane == NZ - 1, pltpu.roll(values, NZ - 1, 1), pltpu.roll(values, 127, 1))


def trace(low, middle, high, sign):
    return low + sign * middle + high


def trace_z(low, middle, high, half):
    return low + middle + high if half else low - middle + high


def one_direction(rates, coefs, index, upper, inflow, speed, size):
    i0, i1, i2 = index
    jump = inflow - upper
    parts = (
        size * jump,
        (-3.0 * speed) * jump - (6.0 * size) * coefs[i1] - (6.0 * speed) * coefs[i2],
        (5.0 * size) * jump + (10.0 * speed) * coefs[i1],
    )
    for i, part in zip(index, parts):
        rates[i] = part if rates[i] is None else rates[i] + part


def transport(place, coefs, inflow_x, j, half):
    rates = [None] * 27
    for b in range(3):
        for c in range(3):
            index = [mode(a, b, c) for a in range(3)]
            upper = trace(*(coefs[i] for i in index), place.sx)
            one_direction(rates, coefs, index, upper, inflow_x[3 * b + c], place.wx, place.ax)
    wy = place.wy(j)
    ay = wy * place.sy
    for a in range(3):
        for c in range(3):
            index = [mode(a, b, c) for b in range(3)]
            upper = trace(*(coefs[i] for i in index), place.sy)
            one_direction(rates, coefs, index, upper, place.from_y(upper), wy, ay)
    wz = place.wz(half)
    az = wz if half else -wz
    for a in range(3):
        for b in range(3):
            index = [mode(a, b, c) for c in range(3)]
            upper = trace_z(*(coefs[i] for i in index), half)
            one_direction(rates, coefs, index, upper, place.from_z(upper, half), wz, az)
    return rates


def velocity_groups(body):
    def step(j, carry):
        for half in range(2):
            carry = body(j, half, pl.multiple_of((2 * j + half) * TILE, TILE), carry)
        return carry

    return step


def load_coefs(field, start):
    return [field[pl.ds(start * 27 + m, TILE, stride=27), :] for m in range(27)]


def moments(place, j, half, values):
    wy = place.wy(j)
    wz = place.wz(half)
    energy = 0.5 * (place.wx * place.wx + wy * wy + wz * wz)
    return [values, place.wx * values, wy * values, wz * values, energy * values]


def stack_rows(rows):
    index = row_index()
    tile = jnp.zeros((TILE, 128), jnp.float32)
    for i, row in enumerate(rows):
        tile = jnp.where(index == i, jnp.broadcast_to(row, (TILE, 128)), tile)
    return tile


def first_kernel(field, rate, halo, planes):
    place = Place()

    def body(j, half, start, sums):
        coefs = load_coefs(field, start)
        for k in range(9):
            halo[pl.ds(k * COUNT + start, TILE), :] = trace(coefs[k], coefs[9 + k], coefs[18 + k], place.sx)
        base = coefs[0]
        out_x = place.ax * trace(base, coefs[9], coefs[18], place.sx)
        upper_y = trace(base, coefs[3], coefs[6], place.sy)
        upper_z = trace_z(base, coefs[1], coefs[2], half)
        wy = place.wy(j)
        wz = place.wz(half)
        kept = (wy * place.sy) * (place.from_y(upper_y) - upper_y) - out_x
        kept = kept + (wz if half else -wz) * (place.from_z(upper_z, half) - upper_z)
        terms = moments(place, j, half, base) + moments(place, j, half, kept) + moments(place, j, half, out_x)
        return tuple(s + t for s, t in zip(sums, terms))

    zero = jnp.zeros((TILE, 128), jnp.float32)
    sums = lax.fori_loop(0, 4, velocity_groups(body), (zero,) * 15)
    sums = [WEIGHT * jnp.sum(s, axis=0, keepdims=True) for s in sums]
    held = stack_rows(sums[:5] + [rate[...]])
    kept = stack_rows(sums[5:10])
    gone = stack_rows(sums[10:])
    for box in range(BOXES):
        second = jnp.where(place.box == box, kept, jnp.where(place.downwind == box, gone, 0.0))
        for q in range(4):
            first = (q * BOXES + box) * ROWS
            planes[first : first + TILE, :] = held
            planes[first + TILE : first + ROWS, :] = second


def second_kernel(field, rate, halo, planes, middle, halo_out, column, upwind_rate):
    place = Place()
    collision = jnp.broadcast_to(rate[...], (TILE, 128))

    def body(j, half, start, carry):
        coefs = load_coefs(field, start)
        inflow = [halo[pl.ds(k * COUNT + start, TILE), :] for k in range(9)]
        rates = transport(place, coefs, inflow, j, half)
        new = [c + STEP * (r - collision * c) for c, r in zip(coefs, rates)]
        for m in range(27):
            middle[pl.ds(m * COUNT + start, TILE), :] = new[m]
        for k in range(9):
            halo_out[pl.ds(k * COUNT + start, TILE), :] = trace(new[k], new[9 + k], new[18 + k], place.sx)
        return carry

    lax.fori_loop(0, 4, velocity_groups(body), 0)

    def of_box(box):
        return sum(planes[pl.ds(pl.multiple_of((q * BOXES + box) * ROWS, ROWS), TILE), :] for q in range(4))

    own = of_box(place.box)
    upwind = of_box(place.upwind)
    kept = sum(planes[p * ROWS + TILE : (p + 1) * ROWS, :] for p in range(4 * BOXES))
    index = row_index()
    first = jnp.where(index < 5, own, pltpu.roll(upwind, 5, 0))
    second = jnp.where(index < 5, kept, pltpu.roll(upwind, 2, 0))
    for p in range(NZ):
        column[p * ROWS : p * ROWS + TILE, :] = first
        column[p * ROWS + TILE : (p + 1) * ROWS, :] = second
    upwind_rate[...] = planes[pl.ds(place.upwind * ROWS + 5, 1), :]


def states(totals):
    density = totals[0]
    flow = [t / density for t in totals[1:4]]
    square = flow[0] * flow[0] + flow[1] * flow[1] + flow[2] * flow[2]
    temper = (2.0 * totals[4] / density - square) / 3.0
    spread = 2.0 * math.pi * temper
    return flow, density / (spread * jnp.sqrt(spread)), 0.5 / temper


def maxwell_moments(state):
    flow, scale, inverse = state
    centres = lax.broadcasted_iota(jnp.int32, (16, 128), 0).astype(jnp.float32) * SPACING + FIRST
    sums = []
    for u in flow:
        offset = centres - u
        bell = jnp.exp(-(offset * offset) * inverse)
        sums.append([jnp.sum(v, axis=0, keepdims=True) for v in (bell, centres * bell, centres * centres * bell)])
    (x0, x1, x2), (y0, y1, y2), (z0, z1, z2) = sums
    scale = WEIGHT * scale
    energy = x2 * y0 * z0 + x0 * y2 * z0 + x0 * y0 * z2
    return [
        scale * (x0 * y0 * z0),
        scale * (x1 * y0 * z0),
        scale * (x0 * y1 * z0),
        scale * (x0 * y0 * z1),
        scale * (0.5 * energy),
    ]


def third_kernel(field, rate, halo, column, upwind_rate, middle, out):
    place = Place()
    first = sum(column[p * ROWS : p * ROWS + TILE, :] for p in range(NZ))
    second = sum(column[p * ROWS + TILE : (p + 1) * ROWS, :] for p in range(NZ))
    row = lambda tile, i: tile[i : i + 1, :]
    nu = rate[...]
    totals = [row(first, i) for i in range(5)]
    flux = [row(second, i) for i in range(5)]
    upwind = [row(first, 5), row(first, 6), row(first, 7), row(second, 5), row(second, 6)]
    now = states(totals)
    gains = maxwell_moments(now)
    later = states([t + STEP * (f - nu * t + nu * g) for t, f, g in zip(totals, flux, gains)])
    before = states(upwind)

    def spread_out(state, factor):
        flow, scale, inverse = state
        wide = lambda v: jnp.broadcast_to(v, (TILE, 128))
        part = (place.wx - flow[0]) * (place.wx - flow[0])
        return wide(part), wide(flow[1]), wide(flow[2]), wide(factor * scale), wide(-inverse)

    now = spread_out(now, STEP * nu)
    before = spread_out(before, STEP * upwind_rate[...])
    later = spread_out(later, nu)
    collision = jnp.broadcast_to(nu, (TILE, 128))

    def body(j, half, start, carry):
        wy = place.wy(j)
        wz = place.wz(half)

        def bell(state):
            part, flow_y, flow_z, scale, inverse = state
            off_y = wy - flow_y
            off_z = wz - flow_z
            return scale * jnp.exp((part + off_y * off_y + off_z * off_z) * inverse)

        coefs = [middle[pl.ds(m * COUNT + start, TILE), :] for m in range(27)]
        coefs[0] = coefs[0] + bell(now)
        inflow = [halo[pl.ds(k * COUNT + start, TILE), :] for k in range(9)]
        inflow[0] = inflow[0] + bell(before)
        rates = transport(place, coefs, inflow, j, half)
        rates[0] = rates[0] + bell(later)
        for m in range(27):
            here = pl.ds(start * 27 + m, TILE, stride=27)
            moved = coefs[m] + STEP * (rates[m] - collision * coefs[m])
            out[here, :] = 0.5 * field[here, :] + 0.5 * moved
        return carry

    lax.fori_loop(0, 4, velocity_groups(body), 0)


def call(kernel, outs, *args):
    vmem = pl.BlockSpec(memory_space=pltpu.VMEM)
    shapes = [jax.ShapeDtypeStruct(s, jnp.float32) for s in outs]
    moved = sum(4 * math.prod(s) for s in outs) + sum(4 * a.size for a in args)
    return pl.pallas_call(
        kernel,
        out_shape=shapes,
        in_specs=[vmem] * len(args),
        out_specs=[vmem] * len(outs),
        cost_estimate=pl.CostEstimate(flops=4000000, bytes_accessed=moved, transcendentals=30000),
    )(*args)


def downwind_pairs():
    pairs = []
    for vel in range(VELS):
        step = 1 if vel >= VELS // 2 else BOXES - 1
        for box in range(BOXES):
            pairs.append((vel * BOXES + box, vel * BOXES + (box + step) % BOXES))
    return pairs


def vel_of(x, z, core):
    return x * 32 + z * 2 + core


PLANES = [
    [vel_of(x, z, core) * BOXES + box for x in range(2) for core in range(2) for box in range(BOXES)]
    for z in range(NZ)
]
COLUMNS = [[vel_of(x, z, core) for z in range(NZ)] for x in range(2) for core in range(2)]


def exchange(blocks, axis, groups):
    count = len(groups[0])
    blocks = blocks.reshape(count, ROWS, 128)
    blocks = lax.all_to_all(blocks, axis, 0, 0, axis_index_groups=groups)
    return blocks.reshape(count * ROWS, 128)


def shards(distribution, collision_rate):
    field = distribution.reshape(COUNT * 27, 128)
    face = (9 * COUNT, 128)
    halo, planes = call(first_kernel, [face, (4 * BOXES * ROWS, 128)], field, collision_rate)
    halo = lax.ppermute(halo, ("vel", "box"), downwind_pairs())
    planes = exchange(planes, ("vel", "box"), PLANES)
    middle, halo, column, upwind_rate = call(
        second_kernel,
        [(27 * COUNT, 128), face, (NZ * ROWS, 128), (1, 128)],
        field,
        collision_rate,
        halo,
        planes,
    )
    halo = lax.ppermute(halo, ("vel", "box"), downwind_pairs())
    column = exchange(column, "vel", COLUMNS)
    (out,) = call(
        third_kernel, [(COUNT * 27, 128)], field, collision_rate, halo, column, upwind_rate, middle
    )
    return out.reshape(distribution.shape)


def solution(mesh):
    return jax.shard_map(
        shards,
        mesh=mesh,
        in_specs=(P("vel", None, None, None, "box", None), P("box", None)),
        out_specs=P("vel", None, None, None, "box", None),
        check_vma=False,
    )
```

```python
import math

import jax
import jax.numpy as jnp
from jax import lax
from jax.experimental import pallas as pl
from jax.experimental.pallas import tpu as pltpu
from jax.sharding import PartitionSpec as P


NZ = 16
VELS = 64
BOXES = 8
COUNT = 64
STEP = 0.02
SPACING = 0.5
FIRST = -3.75
WEIGHT = SPACING**3
ROWS = 16
TILE = 8
GRANT = 16 << 20


def mode(a, b, c):
    return 9 * a + 3 * b + c


def row_index():
    return lax.broadcasted_iota(jnp.int32, (TILE, 128), 0)


class Place:
    def __init__(self):
        self.vel = lax.axis_index("vel")
        self.box = lax.axis_index("box")
        right = self.vel >= VELS // 2
        self.sx = jnp.where(right, 1.0, -1.0)
        self.wx = (self.vel // 4).astype(jnp.float32) * SPACING + FIRST
        self.ax = self.wx * self.sx
        up = self.vel % 4 >= 2
        self.sy = jnp.where(up, 1.0, -1.0)
        self.first_y = (self.vel % 4 * 4).astype(jnp.float32) * SPACING + FIRST
        self.shift_y = jnp.where(up, NZ, 128 - NZ)
        self.upwind = jnp.where(right, (self.box + BOXES - 1) % BOXES, (self.box + 1) % BOXES)
        self.downwind = jnp.where(right, (self.box + 1) % BOXES, (self.box + BOXES - 1) % BOXES)
        self.lane = lax.broadcasted_iota(jnp.int32, (TILE, 128), 1) % NZ

    def wy(self, j):
        return self.first_y + j.astype(jnp.float32) * SPACING

    def wz(self, half):
        return row_index().astype(jnp.float32) * SPACING + (FIRST + half * TILE * SPACING)

    def from_y(self, values):
        return pltpu.roll(values, self.shift_y, 1)

    def from_z(self, values, half):
        if half:
            return jnp.where(self.lane == 0, pltpu.roll(values, 128 + 1 - NZ, 1), pltpu.roll(values, 1, 1))
        return jnp.where(self.lane == NZ - 1, pltpu.roll(values, NZ - 1, 1), pltpu.roll(values, 127, 1))


def trace(low, middle, high, sign):
    return low + sign * middle + high


def trace_z(low, middle, high, half):
    return low + middle + high if half else low - middle + high


def one_direction(rates, coefs, index, upper, inflow, speed, size):
    _, i1, i2 = index
    jump = inflow - upper
    parts = (
        size * jump,
        (-3.0 * speed) * jump - (6.0 * size) * coefs[i1] - (6.0 * speed) * coefs[i2],
        (5.0 * size) * jump + (10.0 * speed) * coefs[i1],
    )
    for i, part in zip(index, parts):
        rates[i] = part if rates[i] is None else rates[i] + part


def transport(place, coefs, inflow_x, j, half):
    rates = [None] * 27
    for b in range(3):
        for c in range(3):
            index = [mode(a, b, c) for a in range(3)]
            upper = trace(*(coefs[i] for i in index), place.sx)
            one_direction(rates, coefs, index, upper, inflow_x[3 * b + c], place.wx, place.ax)
    wy = place.wy(j)
    ay = wy * place.sy
    for a in range(3):
        for c in range(3):
            index = [mode(a, b, c) for b in range(3)]
            upper = trace(*(coefs[i] for i in index), place.sy)
            one_direction(rates, coefs, index, upper, place.from_y(upper), wy, ay)
    wz = place.wz(half)
    az = wz if half else -wz
    for a in range(3):
        for b in range(3):
            index = [mode(a, b, c) for c in range(3)]
            upper = trace_z(*(coefs[i] for i in index), half)
            one_direction(rates, coefs, index, upper, place.from_z(upper, half), wz, az)
    return rates


def velocity_groups(body):
    def step(j, carry):
        for half in range(2):
            carry = body(j, half, pl.multiple_of((2 * j + half) * TILE, TILE), carry)
        return carry

    return step


def load_coefs(field, start):
    return [field[pl.ds(start * 27 + m, TILE, stride=27), :] for m in range(27)]


def moments(place, j, half, values):
    wy = place.wy(j)
    wz = place.wz(half)
    energy = 0.5 * (place.wx * place.wx + wy * wy + wz * wz)
    return [values, place.wx * values, wy * values, wz * values, energy * values]


def stack_rows(rows):
    index = row_index()
    tile = jnp.zeros((TILE, 128), jnp.float32)
    for i, row in enumerate(rows):
        tile = jnp.where(index == i, jnp.broadcast_to(row, (TILE, 128)), tile)
    return tile


def first_kernel(field, rate, halo, planes):
    place = Place()

    def body(j, half, start, sums):
        coefs = load_coefs(field, start)
        for k in range(9):
            halo[pl.ds(k * COUNT + start, TILE), :] = trace(coefs[k], coefs[9 + k], coefs[18 + k], place.sx)
        base = coefs[0]
        out_x = place.ax * trace(base, coefs[9], coefs[18], place.sx)
        upper_y = trace(base, coefs[3], coefs[6], place.sy)
        upper_z = trace_z(base, coefs[1], coefs[2], half)
        wy = place.wy(j)
        wz = place.wz(half)
        kept = (wy * place.sy) * (place.from_y(upper_y) - upper_y) - out_x
        kept = kept + (wz if half else -wz) * (place.from_z(upper_z, half) - upper_z)
        terms = moments(place, j, half, base) + moments(place, j, half, kept) + moments(place, j, half, out_x)
        return tuple(s + t for s, t in zip(sums, terms))

    zero = jnp.zeros((TILE, 128), jnp.float32)
    sums = lax.fori_loop(0, 4, velocity_groups(body), (zero,) * 15)
    sums = [WEIGHT * jnp.sum(s, axis=0, keepdims=True) for s in sums]
    held = stack_rows(sums[:5] + [rate[...]])
    kept = stack_rows(sums[5:10])
    gone = stack_rows(sums[10:])
    for box in range(BOXES):
        second = jnp.where(place.box == box, kept, jnp.where(place.downwind == box, gone, 0.0))
        for q in range(4):
            first = (q * BOXES + box) * ROWS
            planes[first : first + TILE, :] = held
            planes[first + TILE : first + ROWS, :] = second


def second_kernel(field, rate, halo, planes, middle, halo_out, column, upwind_rate):
    place = Place()
    collision = jnp.broadcast_to(rate[...], (TILE, 128))

    def body(j, half, start, carry):
        coefs = load_coefs(field, start)
        inflow = [halo[pl.ds(k * COUNT + start, TILE), :] for k in range(9)]
        rates = transport(place, coefs, inflow, j, half)
        new = [c + STEP * (r - collision * c) for c, r in zip(coefs, rates)]
        for m in range(27):
            middle[pl.ds(m * COUNT + start, TILE), :] = new[m]
        for k in range(9):
            halo_out[pl.ds(k * COUNT + start, TILE), :] = trace(new[k], new[9 + k], new[18 + k], place.sx)
        return carry

    lax.fori_loop(0, 4, velocity_groups(body), 0)

    def of_box(box):
        return sum(planes[pl.ds(pl.multiple_of((q * BOXES + box) * ROWS, ROWS), TILE), :] for q in range(4))

    own = of_box(place.box)
    upwind = of_box(place.upwind)
    kept = sum(planes[p * ROWS + TILE : (p + 1) * ROWS, :] for p in range(4 * BOXES))
    index = row_index()
    first = jnp.where(index < 5, own, pltpu.roll(upwind, 5, 0))
    second = jnp.where(index < 5, kept, pltpu.roll(upwind, 2, 0))
    for p in range(NZ):
        column[p * ROWS : p * ROWS + TILE, :] = first
        column[p * ROWS + TILE : (p + 1) * ROWS, :] = second
    upwind_rate[...] = planes[pl.ds(place.upwind * ROWS + 5, 1), :]


def states(totals):
    density = totals[0]
    flow = [t / density for t in totals[1:4]]
    square = flow[0] * flow[0] + flow[1] * flow[1] + flow[2] * flow[2]
    temper = (2.0 * totals[4] / density - square) / 3.0
    spread = 2.0 * math.pi * temper
    return flow, density / (spread * jnp.sqrt(spread)), 0.5 / temper


def maxwell_moments(state):
    flow, scale, inverse = state
    centres = lax.broadcasted_iota(jnp.int32, (16, 128), 0).astype(jnp.float32) * SPACING + FIRST
    sums = []
    for u in flow:
        offset = centres - u
        bell = jnp.exp(-(offset * offset) * inverse)
        sums.append([jnp.sum(v, axis=0, keepdims=True) for v in (bell, centres * bell, centres * centres * bell)])
    (x0, x1, x2), (y0, y1, y2), (z0, z1, z2) = sums
    scale = WEIGHT * scale
    energy = x2 * y0 * z0 + x0 * y2 * z0 + x0 * y0 * z2
    return [
        scale * (x0 * y0 * z0),
        scale * (x1 * y0 * z0),
        scale * (x0 * y1 * z0),
        scale * (x0 * y0 * z1),
        scale * (0.5 * energy),
    ]


def third_kernel(field, rate, halo, column, upwind_rate, middle, out):
    place = Place()
    first = sum(column[p * ROWS : p * ROWS + TILE, :] for p in range(NZ))
    second = sum(column[p * ROWS + TILE : (p + 1) * ROWS, :] for p in range(NZ))
    row = lambda tile, i: tile[i : i + 1, :]
    nu = rate[...]
    totals = [row(first, i) for i in range(5)]
    flux = [row(second, i) for i in range(5)]
    upwind = [row(first, 5), row(first, 6), row(first, 7), row(second, 5), row(second, 6)]
    now = states(totals)
    gains = maxwell_moments(now)
    later = states([t + STEP * (f - nu * t + nu * g) for t, f, g in zip(totals, flux, gains)])
    before = states(upwind)

    def spread_out(state, factor):
        flow, scale, inverse = state
        wide = lambda v: jnp.broadcast_to(v, (TILE, 128))
        part = (place.wx - flow[0]) * (place.wx - flow[0])
        return wide(part), wide(flow[1]), wide(flow[2]), wide(factor * scale), wide(-inverse)

    now = spread_out(now, STEP * nu)
    before = spread_out(before, STEP * upwind_rate[...])
    later = spread_out(later, nu)
    collision = jnp.broadcast_to(nu, (TILE, 128))

    def body(j, half, start, carry):
        wy = place.wy(j)
        wz = place.wz(half)

        def bell(state):
            part, flow_y, flow_z, scale, inverse = state
            off_y = wy - flow_y
            off_z = wz - flow_z
            return scale * jnp.exp((part + off_y * off_y + off_z * off_z) * inverse)

        coefs = [middle[pl.ds(m * COUNT + start, TILE), :] for m in range(27)]
        coefs[0] = coefs[0] + bell(now)
        inflow = [halo[pl.ds(k * COUNT + start, TILE), :] for k in range(9)]
        inflow[0] = inflow[0] + bell(before)
        rates = transport(place, coefs, inflow, j, half)
        rates[0] = rates[0] + bell(later)
        for m in range(27):
            here = pl.ds(start * 27 + m, TILE, stride=27)
            moved = coefs[m] + STEP * (rates[m] - collision * coefs[m])
            out[here, :] = 0.5 * field[here, :] + 0.5 * moved
        return carry

    lax.fori_loop(0, 4, velocity_groups(body), 0)


def call(kernel, outs, *args):
    vmem = pl.BlockSpec(memory_space=pltpu.VMEM)
    shapes = [jax.ShapeDtypeStruct(s, jnp.float32) for s in outs]
    moved = sum(4 * math.prod(s) for s in outs) + sum(4 * a.size for a in args)
    return pl.pallas_call(
        kernel,
        out_shape=shapes,
        in_specs=[vmem] * len(args),
        out_specs=[vmem] * len(outs),
        compiler_params=pltpu.CompilerParams(vmem_limit_bytes=GRANT),
        cost_estimate=pl.CostEstimate(flops=4000000, bytes_accessed=moved, transcendentals=30000),
    )(*args)


def downwind_pairs():
    pairs = []
    for vel in range(VELS):
        step = 1 if vel >= VELS // 2 else BOXES - 1
        for box in range(BOXES):
            pairs.append((vel * BOXES + box, vel * BOXES + (box + step) % BOXES))
    return pairs


def vel_of(x, z, core):
    return x * 32 + z * 2 + core


PLANES = [
    [vel_of(x, z, core) * BOXES + box for x in range(2) for core in range(2) for box in range(BOXES)]
    for z in range(NZ)
]
COLUMNS = [[vel_of(x, z, core) for z in range(NZ)] for x in range(2) for core in range(2)]


def exchange(blocks, axis, groups):
    count = len(groups[0])
    blocks = blocks.reshape(count, ROWS, 128)
    blocks = lax.all_to_all(blocks, axis, 0, 0, axis_index_groups=groups)
    return blocks.reshape(count * ROWS, 128)


def step(distribution, collision_rate):
    field = distribution.reshape(COUNT * 27, 128)
    face = (9 * COUNT, 128)
    halo, planes = call(first_kernel, [face, (4 * BOXES * ROWS, 128)], field, collision_rate)
    halo = lax.ppermute(halo, ("vel", "box"), downwind_pairs())
    planes = exchange(planes, ("vel", "box"), PLANES)
    middle, halo, column, upwind_rate = call(
        second_kernel,
        [(27 * COUNT, 128), face, (NZ * ROWS, 128), (1, 128)],
        field,
        collision_rate,
        halo,
        planes,
    )
    halo = lax.ppermute(halo, ("vel", "box"), downwind_pairs())
    column = exchange(column, "vel", COLUMNS)
    (out,) = call(
        third_kernel, [(COUNT * 27, 128)], field, collision_rate, halo, column, upwind_rate, middle
    )
    return out.reshape(distribution.shape)


def solution(mesh):
    return jax.shard_map(
        step,
        mesh=mesh,
        in_specs=(P("vel", None, None, None, "box", None), P("box", None)),
        out_specs=P("vel", None, None, None, "box", None),
        check_vma=False,
    )
```

```python
import math

import jax
import jax.numpy as jnp
from jax import lax
from jax.experimental import pallas as pl
from jax.experimental.pallas import tpu as pltpu
from jax.sharding import PartitionSpec as P


NZ = 16
VELS = 64
BOXES = 8
COUNT = 64
STEP = 0.02
SPACING = 0.5
FIRST = -3.75
WEIGHT = SPACING**3
ROWS = 16
TILE = 8
GRANT = 16 << 20
CHUNK = COUNT * 27 // 4


def mode(a, b, c):
    return 9 * a + 3 * b + c


def row_index():
    return lax.broadcasted_iota(jnp.int32, (TILE, 128), 0)


class Place:
    def __init__(self):
        self.vel = lax.axis_index("vel")
        self.box = lax.axis_index("box")
        right = self.vel >= VELS // 2
        self.sx = jnp.where(right, 1.0, -1.0)
        self.wx = (self.vel // 4).astype(jnp.float32) * SPACING + FIRST
        self.ax = self.wx * self.sx
        up = self.vel % 4 >= 2
        self.sy = jnp.where(up, 1.0, -1.0)
        self.first_y = (self.vel % 4 * 4).astype(jnp.float32) * SPACING + FIRST
        self.shift_y = jnp.where(up, NZ, 128 - NZ)
        self.upwind = jnp.where(right, (self.box + BOXES - 1) % BOXES, (self.box + 1) % BOXES)
        self.downwind = jnp.where(right, (self.box + 1) % BOXES, (self.box + BOXES - 1) % BOXES)
        self.lane = lax.broadcasted_iota(jnp.int32, (TILE, 128), 1) % NZ

    def wy(self, j):
        return self.first_y + j.astype(jnp.float32) * SPACING

    def wz(self, half):
        return row_index().astype(jnp.float32) * SPACING + (FIRST + half * TILE * SPACING)

    def from_y(self, values):
        return pltpu.roll(values, self.shift_y, 1)

    def from_z(self, values, half):
        if half:
            return jnp.where(self.lane == 0, pltpu.roll(values, 128 + 1 - NZ, 1), pltpu.roll(values, 1, 1))
        return jnp.where(self.lane == NZ - 1, pltpu.roll(values, NZ - 1, 1), pltpu.roll(values, 127, 1))


def trace(low, middle, high, sign):
    return low + sign * middle + high


def trace_z(low, middle, high, half):
    return low + middle + high if half else low - middle + high


def one_direction(rates, coefs, index, upper, inflow, speed, size):
    _, i1, i2 = index
    jump = inflow - upper
    parts = (
        size * jump,
        (-3.0 * speed) * jump - (6.0 * size) * coefs[i1] - (6.0 * speed) * coefs[i2],
        (5.0 * size) * jump + (10.0 * speed) * coefs[i1],
    )
    for i, part in zip(index, parts):
        rates[i] = part if rates[i] is None else rates[i] + part


def transport(place, coefs, inflow_x, j, half):
    rates = [None] * 27
    for b in range(3):
        for c in range(3):
            index = [mode(a, b, c) for a in range(3)]
            upper = trace(*(coefs[i] for i in index), place.sx)
            one_direction(rates, coefs, index, upper, inflow_x[3 * b + c], place.wx, place.ax)
    wy = place.wy(j)
    ay = wy * place.sy
    for a in range(3):
        for c in range(3):
            index = [mode(a, b, c) for b in range(3)]
            upper = trace(*(coefs[i] for i in index), place.sy)
            one_direction(rates, coefs, index, upper, place.from_y(upper), wy, ay)
    wz = place.wz(half)
    az = wz if half else -wz
    for a in range(3):
        for b in range(3):
            index = [mode(a, b, c) for c in range(3)]
            upper = trace_z(*(coefs[i] for i in index), half)
            one_direction(rates, coefs, index, upper, place.from_z(upper, half), wz, az)
    return rates


def velocity_groups(body):
    def step(j, carry):
        for half in range(2):
            carry = body(j, half, pl.multiple_of((2 * j + half) * TILE, TILE), carry)
        return carry

    return step


def load_coefs(field, start):
    return [field[pl.ds(start * 27 + m, TILE, stride=27), :] for m in range(27)]


def moments(place, j, half, values):
    wy = place.wy(j)
    wz = place.wz(half)
    energy = 0.5 * (place.wx * place.wx + wy * wy + wz * wz)
    return [values, place.wx * values, wy * values, wz * values, energy * values]


def stack_rows(rows):
    index = row_index()
    tile = jnp.zeros((TILE, 128), jnp.float32)
    for i, row in enumerate(rows):
        tile = jnp.where(index == i, jnp.broadcast_to(row, (TILE, 128)), tile)
    return tile


def chunk_copy(source, target, sems, j):
    rows = pl.ds(pl.multiple_of(j * CHUNK, CHUNK), CHUNK)
    return pltpu.make_async_copy(source.at[rows], target.at[rows], sems.at[j])


def first_kernel(field_hbm, rate_hbm, halo, planes, field, rate, sems):
    place = Place()
    for j in range(4):
        chunk_copy(field_hbm, field, sems, j).start()
    rate_copy = pltpu.make_async_copy(rate_hbm, rate, sems.at[4])
    rate_copy.start()

    def body(j, half, start, sums):
        if not half:
            chunk_copy(field_hbm, field, sems, j).wait()
        coefs = load_coefs(field, start)
        for k in range(9):
            halo[pl.ds(k * COUNT + start, TILE), :] = trace(coefs[k], coefs[9 + k], coefs[18 + k], place.sx)
        base = coefs[0]
        out_x = place.ax * trace(base, coefs[9], coefs[18], place.sx)
        upper_y = trace(base, coefs[3], coefs[6], place.sy)
        upper_z = trace_z(base, coefs[1], coefs[2], half)
        wy = place.wy(j)
        wz = place.wz(half)
        kept = (wy * place.sy) * (place.from_y(upper_y) - upper_y) - out_x
        kept = kept + (wz if half else -wz) * (place.from_z(upper_z, half) - upper_z)
        terms = moments(place, j, half, base) + moments(place, j, half, kept) + moments(place, j, half, out_x)
        return tuple(s + t for s, t in zip(sums, terms))

    zero = jnp.zeros((TILE, 128), jnp.float32)
    sums = lax.fori_loop(0, 4, velocity_groups(body), (zero,) * 15)
    rate_copy.wait()
    sums = [WEIGHT * jnp.sum(s, axis=0, keepdims=True) for s in sums]
    held = stack_rows(sums[:5] + [rate[...]])
    kept = stack_rows(sums[5:10])
    gone = stack_rows(sums[10:])
    for box in range(BOXES):
        second = jnp.where(place.box == box, kept, jnp.where(place.downwind == box, gone, 0.0))
        for q in range(4):
            first = (q * BOXES + box) * ROWS
            planes[first : first + TILE, :] = held
            planes[first + TILE : first + ROWS, :] = second


def second_kernel(field, rate, halo, planes, middle, halo_out, column, upwind_rate):
    place = Place()
    collision = jnp.broadcast_to(rate[...], (TILE, 128))

    def body(j, half, start, carry):
        coefs = load_coefs(field, start)
        inflow = [halo[pl.ds(k * COUNT + start, TILE), :] for k in range(9)]
        rates = transport(place, coefs, inflow, j, half)
        new = [c + STEP * (r - collision * c) for c, r in zip(coefs, rates)]
        for m in range(27):
            middle[pl.ds(m * COUNT + start, TILE), :] = new[m]
        for k in range(9):
            halo_out[pl.ds(k * COUNT + start, TILE), :] = trace(new[k], new[9 + k], new[18 + k], place.sx)
        return carry

    lax.fori_loop(0, 4, velocity_groups(body), 0)

    def of_box(box):
        return sum(planes[pl.ds(pl.multiple_of((q * BOXES + box) * ROWS, ROWS), TILE), :] for q in range(4))

    own = of_box(place.box)
    upwind = of_box(place.upwind)
    kept = sum(planes[p * ROWS + TILE : (p + 1) * ROWS, :] for p in range(4 * BOXES))
    index = row_index()
    first = jnp.where(index < 5, own, pltpu.roll(upwind, 5, 0))
    second = jnp.where(index < 5, kept, pltpu.roll(upwind, 2, 0))
    for p in range(NZ):
        column[p * ROWS : p * ROWS + TILE, :] = first
        column[p * ROWS + TILE : (p + 1) * ROWS, :] = second
    upwind_rate[...] = planes[pl.ds(place.upwind * ROWS + 5, 1), :]


def states(totals):
    density = totals[0]
    flow = [t / density for t in totals[1:4]]
    square = flow[0] * flow[0] + flow[1] * flow[1] + flow[2] * flow[2]
    temper = (2.0 * totals[4] / density - square) / 3.0
    spread = 2.0 * math.pi * temper
    return flow, density / (spread * jnp.sqrt(spread)), 0.5 / temper


def maxwell_moments(state):
    flow, scale, inverse = state
    centres = lax.broadcasted_iota(jnp.int32, (16, 128), 0).astype(jnp.float32) * SPACING + FIRST
    sums = []
    for u in flow:
        offset = centres - u
        bell = jnp.exp(-(offset * offset) * inverse)
        sums.append([jnp.sum(v, axis=0, keepdims=True) for v in (bell, centres * bell, centres * centres * bell)])
    (x0, x1, x2), (y0, y1, y2), (z0, z1, z2) = sums
    scale = WEIGHT * scale
    energy = x2 * y0 * z0 + x0 * y2 * z0 + x0 * y0 * z2
    return [
        scale * (x0 * y0 * z0),
        scale * (x1 * y0 * z0),
        scale * (x0 * y1 * z0),
        scale * (x0 * y0 * z1),
        scale * (0.5 * energy),
    ]


def third_kernel(field, rate, halo, column, upwind_rate, middle, out_hbm, out, sems):
    place = Place()
    first = sum(column[p * ROWS : p * ROWS + TILE, :] for p in range(NZ))
    second = sum(column[p * ROWS + TILE : (p + 1) * ROWS, :] for p in range(NZ))
    row = lambda tile, i: tile[i : i + 1, :]
    nu = rate[...]
    totals = [row(first, i) for i in range(5)]
    flux = [row(second, i) for i in range(5)]
    upwind = [row(first, 5), row(first, 6), row(first, 7), row(second, 5), row(second, 6)]
    now = states(totals)
    gains = maxwell_moments(now)
    later = states([t + STEP * (f - nu * t + nu * g) for t, f, g in zip(totals, flux, gains)])
    before = states(upwind)

    def spread_out(state, factor):
        flow, scale, inverse = state
        wide = lambda v: jnp.broadcast_to(v, (TILE, 128))
        part = (place.wx - flow[0]) * (place.wx - flow[0])
        return wide(part), wide(flow[1]), wide(flow[2]), wide(factor * scale), wide(-inverse)

    now = spread_out(now, STEP * nu)
    before = spread_out(before, STEP * upwind_rate[...])
    later = spread_out(later, nu)
    collision = jnp.broadcast_to(nu, (TILE, 128))

    def body(j, half, start, carry):
        wy = place.wy(j)
        wz = place.wz(half)

        def bell(state):
            part, flow_y, flow_z, scale, inverse = state
            off_y = wy - flow_y
            off_z = wz - flow_z
            return scale * jnp.exp((part + off_y * off_y + off_z * off_z) * inverse)

        coefs = [middle[pl.ds(m * COUNT + start, TILE), :] for m in range(27)]
        coefs[0] = coefs[0] + bell(now)
        inflow = [halo[pl.ds(k * COUNT + start, TILE), :] for k in range(9)]
        inflow[0] = inflow[0] + bell(before)
        rates = transport(place, coefs, inflow, j, half)
        rates[0] = rates[0] + bell(later)
        for m in range(27):
            here = pl.ds(start * 27 + m, TILE, stride=27)
            moved = coefs[m] + STEP * (rates[m] - collision * coefs[m])
            out[here, :] = 0.5 * field[here, :] + 0.5 * moved
        if half:
            chunk_copy(out, out_hbm, sems, j).start()
        return carry

    lax.fori_loop(0, 4, velocity_groups(body), 0)
    for j in range(4):
        chunk_copy(out, out_hbm, sems, j).wait()


def call(kernel, outs, *args, remote_in=0, remote_out=False, scratch=()):
    vmem = pl.BlockSpec(memory_space=pltpu.VMEM)
    hbm = pl.BlockSpec(memory_space=pltpu.HBM)
    shapes = [jax.ShapeDtypeStruct(s, jnp.float32) for s in outs]
    moved = sum(4 * math.prod(s) for s in outs) + sum(4 * a.size for a in args)
    return pl.pallas_call(
        kernel,
        out_shape=shapes,
        in_specs=[hbm] * remote_in + [vmem] * (len(args) - remote_in),
        out_specs=[hbm if remote_out else vmem] * len(outs),
        scratch_shapes=scratch,
        compiler_params=pltpu.CompilerParams(vmem_limit_bytes=GRANT),
        cost_estimate=pl.CostEstimate(flops=4000000, bytes_accessed=moved, transcendentals=30000),
    )(*args)


def downwind_pairs():
    pairs = []
    for vel in range(VELS):
        step = 1 if vel >= VELS // 2 else BOXES - 1
        for box in range(BOXES):
            pairs.append((vel * BOXES + box, vel * BOXES + (box + step) % BOXES))
    return pairs


def vel_of(x, z, core):
    return x * 32 + z * 2 + core


PLANES = [
    [vel_of(x, z, core) * BOXES + box for x in range(2) for core in range(2) for box in range(BOXES)]
    for z in range(NZ)
]
COLUMNS = [[vel_of(x, z, core) for z in range(NZ)] for x in range(2) for core in range(2)]


def exchange(blocks, axis, groups):
    count = len(groups[0])
    blocks = blocks.reshape(count, ROWS, 128)
    blocks = lax.all_to_all(blocks, axis, 0, 0, axis_index_groups=groups)
    return blocks.reshape(count * ROWS, 128)


def step(distribution, collision_rate):
    field = pltpu.with_memory_space_constraint(distribution.reshape(COUNT * 27, 128), pltpu.HBM)
    collision_rate = pltpu.with_memory_space_constraint(collision_rate, pltpu.HBM)
    face = (9 * COUNT, 128)
    whole = (27 * COUNT, 128)
    halo, planes, field, rate = call(
        first_kernel,
        [face, (4 * BOXES * ROWS, 128), whole, (1, 128)],
        field,
        collision_rate,
        remote_in=2,
        scratch=[pltpu.SemaphoreType.DMA((5,))],
    )
    halo = lax.ppermute(halo, ("vel", "box"), downwind_pairs())
    planes = exchange(planes, ("vel", "box"), PLANES)
    middle, halo, column, upwind_rate = call(
        second_kernel,
        [whole, face, (NZ * ROWS, 128), (1, 128)],
        field,
        rate,
        halo,
        planes,
    )
    halo = lax.ppermute(halo, ("vel", "box"), downwind_pairs())
    column = exchange(column, "vel", COLUMNS)
    (out,) = call(
        third_kernel,
        [whole],
        field,
        rate,
        halo,
        column,
        upwind_rate,
        middle,
        remote_out=True,
        scratch=[pltpu.VMEM(whole, jnp.float32), pltpu.SemaphoreType.DMA((4,))],
    )
    return out.reshape(distribution.shape)


def solution(mesh):
    return jax.shard_map(
        step,
        mesh=mesh,
        in_specs=(P("vel", None, None, None, "box", None), P("box", None)),
        out_specs=P("vel", None, None, None, "box", None),
        check_vma=False,
    )
```

```python
import math

import jax
import jax.numpy as jnp
from jax import lax
from jax.experimental import pallas as pl
from jax.experimental.pallas import tpu as pltpu
from jax.sharding import PartitionSpec as P


NZ = 16
VELS = 64
BOXES = 8
COUNT = 64
STEP = 0.02
SPACING = 0.5
FIRST = -3.75
WEIGHT = SPACING**3
ROWS = 16
TILE = 8
GRANT = 16 << 20
CHUNK = COUNT * 27 // 4


def mode(a, b, c):
    return 9 * a + 3 * b + c


def row_index():
    return lax.broadcasted_iota(jnp.int32, (TILE, 128), 0)


class Place:
    def __init__(self):
        self.vel = lax.axis_index("vel")
        self.box = lax.axis_index("box")
        right = self.vel >= VELS // 2
        self.sx = jnp.where(right, 1.0, -1.0)
        self.wx = (self.vel // 4).astype(jnp.float32) * SPACING + FIRST
        self.ax = self.wx * self.sx
        up = self.vel % 4 >= 2
        self.sy = jnp.where(up, 1.0, -1.0)
        self.first_y = (self.vel % 4 * 4).astype(jnp.float32) * SPACING + FIRST
        self.shift_y = jnp.where(up, NZ, 128 - NZ)
        self.upwind = jnp.where(right, (self.box + BOXES - 1) % BOXES, (self.box + 1) % BOXES)
        self.downwind = jnp.where(right, (self.box + 1) % BOXES, (self.box + BOXES - 1) % BOXES)
        self.lane = lax.broadcasted_iota(jnp.int32, (TILE, 128), 1) % NZ

    def wy(self, j):
        return self.first_y + j.astype(jnp.float32) * SPACING

    def wz(self, half):
        return row_index().astype(jnp.float32) * SPACING + (FIRST + half * TILE * SPACING)

    def from_y(self, values):
        return pltpu.roll(values, self.shift_y, 1)

    def from_z(self, values, half):
        if half:
            return jnp.where(self.lane == 0, pltpu.roll(values, 128 + 1 - NZ, 1), pltpu.roll(values, 1, 1))
        return jnp.where(self.lane == NZ - 1, pltpu.roll(values, NZ - 1, 1), pltpu.roll(values, 127, 1))


def trace(low, middle, high, sign):
    return low + sign * middle + high


def trace_z(low, middle, high, half):
    return low + middle + high if half else low - middle + high


def one_direction(rates, coefs, index, upper, inflow, speed, size):
    _, i1, i2 = index
    jump = inflow - upper
    parts = (
        size * jump,
        (-3.0 * speed) * jump - (6.0 * size) * coefs[i1] - (6.0 * speed) * coefs[i2],
        (5.0 * size) * jump + (10.0 * speed) * coefs[i1],
    )
    for i, part in zip(index, parts):
        rates[i] = part if rates[i] is None else rates[i] + part


def transport(place, coefs, inflow_x, j, half):
    rates = [None] * 27
    for b in range(3):
        for c in range(3):
            index = [mode(a, b, c) for a in range(3)]
            upper = trace(*(coefs[i] for i in index), place.sx)
            one_direction(rates, coefs, index, upper, inflow_x[3 * b + c], place.wx, place.ax)
    wy = place.wy(j)
    ay = wy * place.sy
    for a in range(3):
        for c in range(3):
            index = [mode(a, b, c) for b in range(3)]
            upper = trace(*(coefs[i] for i in index), place.sy)
            one_direction(rates, coefs, index, upper, place.from_y(upper), wy, ay)
    wz = place.wz(half)
    az = wz if half else -wz
    for a in range(3):
        for b in range(3):
            index = [mode(a, b, c) for c in range(3)]
            upper = trace_z(*(coefs[i] for i in index), half)
            one_direction(rates, coefs, index, upper, place.from_z(upper, half), wz, az)
    return rates


def velocity_groups(body):
    def step(j, carry):
        for half in range(2):
            carry = body(j, half, pl.multiple_of((2 * j + half) * TILE, TILE), carry)
        return carry

    return step


def load_coefs(field, start):
    return [field[pl.ds(start * 27 + m, TILE, stride=27), :] for m in range(27)]


def moments(place, j, half, values):
    wy = place.wy(j)
    wz = place.wz(half)
    energy = 0.5 * (place.wx * place.wx + wy * wy + wz * wz)
    return [values, place.wx * values, wy * values, wz * values, energy * values]


def stack_rows(rows):
    index = row_index()
    tile = jnp.zeros((TILE, 128), jnp.float32)
    for i, row in enumerate(rows):
        tile = jnp.where(index == i, jnp.broadcast_to(row, (TILE, 128)), tile)
    return tile


def chunk_copy(source, target, sems, j):
    rows = pl.ds(pl.multiple_of(j * CHUNK, CHUNK), CHUNK)
    return pltpu.make_async_copy(source.at[rows], target.at[rows], sems.at[j])


def first_kernel(field_hbm, rate_hbm, halo, column, field, rate, sems):
    place = Place()
    for j in range(4):
        chunk_copy(field_hbm, field, sems, j).start()
    rate_copy = pltpu.make_async_copy(rate_hbm, rate, sems.at[4])
    rate_copy.start()

    def body(j, half, start, sums):
        if not half:
            chunk_copy(field_hbm, field, sems, j).wait()
        coefs = load_coefs(field, start)
        for k in range(9):
            halo[pl.ds(k * COUNT + start, TILE), :] = trace(coefs[k], coefs[9 + k], coefs[18 + k], place.sx)
        base = coefs[0]
        out_x = place.ax * trace(base, coefs[9], coefs[18], place.sx)
        upper_y = trace(base, coefs[3], coefs[6], place.sy)
        upper_z = trace_z(base, coefs[1], coefs[2], half)
        wy = place.wy(j)
        wz = place.wz(half)
        kept = (wy * place.sy) * (place.from_y(upper_y) - upper_y) - out_x
        kept = kept + (wz if half else -wz) * (place.from_z(upper_z, half) - upper_z)
        terms = moments(place, j, half, base) + moments(place, j, half, kept) + moments(place, j, half, out_x)
        return tuple(s + t for s, t in zip(sums, terms))

    zero = jnp.zeros((TILE, 128), jnp.float32)
    sums = lax.fori_loop(0, 4, velocity_groups(body), (zero,) * 15)
    sums = [WEIGHT * jnp.sum(s, axis=0, keepdims=True) for s in sums]
    first = stack_rows(sums[:5] + sums[10:13])
    second = stack_rows(sums[5:10] + sums[13:])
    for p in range(NZ):
        column[p * ROWS : p * ROWS + TILE, :] = first
        column[p * ROWS + TILE : (p + 1) * ROWS, :] = second
    rate_copy.wait()


def between_kernel(column, rate, planes):
    place = Place()
    first = sum(column[p * ROWS : p * ROWS + TILE, :] for p in range(NZ))
    second = sum(column[p * ROWS + TILE : (p + 1) * ROWS, :] for p in range(NZ))
    index = row_index()
    held = jnp.where(index < 5, first, jnp.broadcast_to(rate[...], (TILE, 128)))
    gone = jnp.where(index < 3, pltpu.roll(first, 3, 0), pltpu.roll(second, TILE - 2, 0))
    for box in range(BOXES):
        sent = jnp.where(place.box == box, second, jnp.where(place.downwind == box, gone, 0.0))
        for q in range(4):
            start = (q * BOXES + box) * ROWS
            planes[start : start + TILE, :] = held
            planes[start + TILE : start + ROWS, :] = sent


def second_kernel(field, rate, halo, middle, halo_out):
    place = Place()
    collision = jnp.broadcast_to(rate[...], (TILE, 128))

    def body(j, half, start, carry):
        coefs = load_coefs(field, start)
        inflow = [halo[pl.ds(k * COUNT + start, TILE), :] for k in range(9)]
        rates = transport(place, coefs, inflow, j, half)
        new = [c + STEP * (r - collision * c) for c, r in zip(coefs, rates)]
        for m in range(27):
            middle[pl.ds(m * COUNT + start, TILE), :] = new[m]
        for k in range(9):
            halo_out[pl.ds(k * COUNT + start, TILE), :] = trace(new[k], new[9 + k], new[18 + k], place.sx)
        return carry

    lax.fori_loop(0, 4, velocity_groups(body), 0)


def states(totals):
    density = totals[0]
    flow = [t / density for t in totals[1:4]]
    square = flow[0] * flow[0] + flow[1] * flow[1] + flow[2] * flow[2]
    temper = (2.0 * totals[4] / density - square) / 3.0
    spread = 2.0 * math.pi * temper
    return flow, density / (spread * jnp.sqrt(spread)), 0.5 / temper


def maxwell_moments(state):
    flow, scale, inverse = state
    centres = lax.broadcasted_iota(jnp.int32, (16, 128), 0).astype(jnp.float32) * SPACING + FIRST
    sums = []
    for u in flow:
        offset = centres - u
        bell = jnp.exp(-(offset * offset) * inverse)
        sums.append([jnp.sum(v, axis=0, keepdims=True) for v in (bell, centres * bell, centres * centres * bell)])
    (x0, x1, x2), (y0, y1, y2), (z0, z1, z2) = sums
    scale = WEIGHT * scale
    energy = x2 * y0 * z0 + x0 * y2 * z0 + x0 * y0 * z2
    return [
        scale * (x0 * y0 * z0),
        scale * (x1 * y0 * z0),
        scale * (x0 * y1 * z0),
        scale * (x0 * y0 * z1),
        scale * (0.5 * energy),
    ]


def third_kernel(field, rate, halo, planes, middle, out_hbm, out, sems):
    place = Place()

    def of_box(box):
        return sum(planes[pl.ds(pl.multiple_of((q * BOXES + box) * ROWS, ROWS), TILE), :] for q in range(4))

    own = of_box(place.box)
    behind = of_box(place.upwind)
    kept = sum(planes[p * ROWS + TILE : (p + 1) * ROWS, :] for p in range(4 * BOXES))
    nu = rate[...]
    upwind_nu = planes[pl.ds(place.upwind * ROWS + 5, 1), :]
    totals, upwind, flux = ([tile[i : i + 1, :] for i in range(5)] for tile in (own, behind, kept))
    now = states(totals)
    gains = maxwell_moments(now)
    later = states([t + STEP * (f - nu * t + nu * g) for t, f, g in zip(totals, flux, gains)])
    before = states(upwind)

    def spread_out(state, factor):
        flow, scale, inverse = state
        wide = lambda v: jnp.broadcast_to(v, (TILE, 128))
        part = (place.wx - flow[0]) * (place.wx - flow[0])
        return wide(part), wide(flow[1]), wide(flow[2]), wide(factor * scale), wide(-inverse)

    now = spread_out(now, STEP * nu)
    before = spread_out(before, STEP * upwind_nu)
    later = spread_out(later, nu)
    collision = jnp.broadcast_to(nu, (TILE, 128))

    def body(j, half, start, carry):
        wy = place.wy(j)
        wz = place.wz(half)

        def bell(state):
            part, flow_y, flow_z, scale, inverse = state
            off_y = wy - flow_y
            off_z = wz - flow_z
            return scale * jnp.exp((part + off_y * off_y + off_z * off_z) * inverse)

        coefs = [middle[pl.ds(m * COUNT + start, TILE), :] for m in range(27)]
        coefs[0] = coefs[0] + bell(now)
        inflow = [halo[pl.ds(k * COUNT + start, TILE), :] for k in range(9)]
        inflow[0] = inflow[0] + bell(before)
        rates = transport(place, coefs, inflow, j, half)
        rates[0] = rates[0] + bell(later)
        for m in range(27):
            here = pl.ds(start * 27 + m, TILE, stride=27)
            moved = coefs[m] + STEP * (rates[m] - collision * coefs[m])
            out[here, :] = 0.5 * field[here, :] + 0.5 * moved
        if half:
            chunk_copy(out, out_hbm, sems, j).start()
        return carry

    lax.fori_loop(0, 4, velocity_groups(body), 0)
    for j in range(4):
        chunk_copy(out, out_hbm, sems, j).wait()


def call(kernel, outs, *args, remote_in=0, remote_out=False, scratch=()):
    vmem = pl.BlockSpec(memory_space=pltpu.VMEM)
    hbm = pl.BlockSpec(memory_space=pltpu.HBM)
    shapes = [jax.ShapeDtypeStruct(s, jnp.float32) for s in outs]
    moved = sum(4 * math.prod(s) for s in outs) + sum(4 * a.size for a in args)
    return pl.pallas_call(
        kernel,
        out_shape=shapes,
        in_specs=[hbm] * remote_in + [vmem] * (len(args) - remote_in),
        out_specs=[hbm if remote_out else vmem] * len(outs),
        scratch_shapes=scratch,
        compiler_params=pltpu.CompilerParams(vmem_limit_bytes=GRANT),
        cost_estimate=pl.CostEstimate(flops=4000000, bytes_accessed=moved, transcendentals=30000),
    )(*args)


def downwind_pairs():
    pairs = []
    for vel in range(VELS):
        step = 1 if vel >= VELS // 2 else BOXES - 1
        for box in range(BOXES):
            pairs.append((vel * BOXES + box, vel * BOXES + (box + step) % BOXES))
    return pairs


def vel_of(x, z, core):
    return x * 32 + z * 2 + core


PLANES = [
    [vel_of(x, z, core) * BOXES + box for x in range(2) for core in range(2) for box in range(BOXES)]
    for z in range(NZ)
]
COLUMNS = [[vel_of(x, (z + 8) % NZ, core) for z in range(NZ)] for x in range(2) for core in range(2)]


def exchange(blocks, axis, groups):
    count = len(groups[0])
    blocks = blocks.reshape(count, ROWS, 128)
    blocks = lax.all_to_all(blocks, axis, 0, 0, axis_index_groups=groups)
    return blocks.reshape(count * ROWS, 128)


def step(distribution, collision_rate):
    field = pltpu.with_memory_space_constraint(distribution.reshape(COUNT * 27, 128), pltpu.HBM)
    collision_rate = pltpu.with_memory_space_constraint(collision_rate, pltpu.HBM)
    face = (9 * COUNT, 128)
    whole = (27 * COUNT, 128)
    halo, column, field, rate = call(
        first_kernel,
        [face, (NZ * ROWS, 128), whole, (1, 128)],
        field,
        collision_rate,
        remote_in=2,
        scratch=[pltpu.SemaphoreType.DMA((5,))],
    )
    halo = lax.ppermute(halo, ("vel", "box"), downwind_pairs())
    column = exchange(column, "vel", COLUMNS)
    middle, halo = call(second_kernel, [whole, face], field, rate, halo)
    halo = lax.ppermute(halo, ("vel", "box"), downwind_pairs())
    (planes,) = call(between_kernel, [(4 * BOXES * ROWS, 128)], column, rate)
    planes = exchange(planes, ("vel", "box"), PLANES)
    (out,) = call(
        third_kernel,
        [whole],
        field,
        rate,
        halo,
        planes,
        middle,
        remote_out=True,
        scratch=[pltpu.VMEM(whole, jnp.float32), pltpu.SemaphoreType.DMA((4,))],
    )
    return out.reshape(distribution.shape)


def solution(mesh):
    return jax.shard_map(
        step,
        mesh=mesh,
        in_specs=(P("vel", None, None, None, "box", None), P("box", None)),
        out_specs=P("vel", None, None, None, "box", None),
        check_vma=False,
    )
```

```python
import math

import jax
import jax.numpy as jnp
from jax import lax
from jax.experimental import pallas as pl
from jax.experimental.pallas import tpu as pltpu
from jax.sharding import PartitionSpec as P


NZ = 16
VPD = 16
VELS = 64
LEAD = 8
BOXES = 8
COUNT = 64
STEP = 0.02
SPACING = 0.5
FIRST = -3.75
WEIGHT = SPACING**3
COLUMN_ROWS = 12
PLANE_ROWS = 10
TILE = 8
GRANT = 16 << 20
CHUNK = COUNT * 27 // 4
FACE = 9 * COUNT + TILE


def mode(a, b, c):
    return 9 * a + 3 * b + c


def row_index():
    return lax.broadcasted_iota(jnp.int32, (TILE, 128), 0)


class Place:
    def __init__(self):
        self.vel = lax.axis_index("vel")
        self.box = lax.axis_index("box")
        right = self.vel >= VELS // 2
        self.sx = jnp.where(right, 1.0, -1.0)
        self.wx = (self.vel // 4).astype(jnp.float32) * SPACING + FIRST
        self.ax = self.wx * self.sx
        up = self.vel % 4 >= 2
        self.sy = jnp.where(up, 1.0, -1.0)
        self.first_y = (self.vel % 4 * 4).astype(jnp.float32) * SPACING + FIRST
        self.shift_y = jnp.where(up, NZ, 128 - NZ)
        self.upwind = jnp.where(right, (self.box + BOXES - 1) % BOXES, (self.box + 1) % BOXES)
        self.downwind = jnp.where(right, (self.box + 1) % BOXES, (self.box + BOXES - 1) % BOXES)
        self.lane = lax.broadcasted_iota(jnp.int32, (TILE, 128), 1) % NZ

    def wy(self, j):
        return self.first_y + j.astype(jnp.float32) * SPACING

    def wz(self, half):
        return row_index().astype(jnp.float32) * SPACING + (FIRST + half * TILE * SPACING)

    def from_y(self, values):
        return pltpu.roll(values, self.shift_y, 1)

    def from_z(self, values, half):
        if half:
            return jnp.where(self.lane == 0, pltpu.roll(values, 128 + 1 - NZ, 1), pltpu.roll(values, 1, 1))
        return jnp.where(self.lane == NZ - 1, pltpu.roll(values, NZ - 1, 1), pltpu.roll(values, 127, 1))


def trace(low, middle, high, sign):
    return low + sign * middle + high


def trace_z(low, middle, high, half):
    return low + middle + high if half else low - middle + high


def one_direction(rates, coefs, index, upper, inflow, speed, size):
    _, i1, i2 = index
    jump = inflow - upper
    parts = (
        size * jump,
        (-3.0 * speed) * jump - (6.0 * size) * coefs[i1] - (6.0 * speed) * coefs[i2],
        (5.0 * size) * jump + (10.0 * speed) * coefs[i1],
    )
    for i, part in zip(index, parts):
        rates[i] = part if rates[i] is None else rates[i] + part


def transport(place, coefs, inflow_x, j, half):
    rates = [None] * 27
    for b in range(3):
        for c in range(3):
            index = [mode(a, b, c) for a in range(3)]
            upper = trace(*(coefs[i] for i in index), place.sx)
            one_direction(rates, coefs, index, upper, inflow_x[3 * b + c], place.wx, place.ax)
    wy = place.wy(j)
    ay = wy * place.sy
    for a in range(3):
        for c in range(3):
            index = [mode(a, b, c) for b in range(3)]
            upper = trace(*(coefs[i] for i in index), place.sy)
            one_direction(rates, coefs, index, upper, place.from_y(upper), wy, ay)
    wz = place.wz(half)
    az = wz if half else -wz
    for a in range(3):
        for b in range(3):
            index = [mode(a, b, c) for c in range(3)]
            upper = trace_z(*(coefs[i] for i in index), half)
            one_direction(rates, coefs, index, upper, place.from_z(upper, half), wz, az)
    return rates


def velocity_groups(body):
    def step(j, carry):
        for half in range(2):
            carry = body(j, half, pl.multiple_of((2 * j + half) * TILE, TILE), carry)
        return carry

    return step


def load_coefs(field, start):
    return [field[pl.ds(start * 27 + m, TILE, stride=27), :] for m in range(27)]


def moments(place, j, half, values):
    wy = place.wy(j)
    wz = place.wz(half)
    return [values, wy * values, wz * values, (0.5 * (wy * wy + wz * wz)) * values]


def all_moments(wx, four):
    total = lambda values: jnp.sum(values, axis=0, keepdims=True)
    count, along_y, along_z, energy = four
    return [
        total(count),
        total(wx * count),
        total(along_y),
        total(along_z),
        total(energy + (0.5 * (wx * wx)) * count),
    ]


def chunk_copy(source, target, sems, j, size=CHUNK):
    rows = pl.ds(pl.multiple_of(j * size, size), size)
    return pltpu.make_async_copy(source.at[rows], target.at[rows], sems.at[j])


def first_kernel(field_hbm, rate_hbm, halo, column, field, rate, sems):
    place = Place()
    for j in range(4):
        chunk_copy(field_hbm, field, sems, j).start()
    rate_copy = pltpu.make_async_copy(rate_hbm, rate, sems.at[4])
    rate_copy.start()

    def body(j, half, start, sums):
        if not half:
            chunk_copy(field_hbm, field, sems, j).wait()
        coefs = load_coefs(field, start)
        for k in range(9):
            halo[pl.ds(k * COUNT + start, TILE), :] = trace(coefs[k], coefs[9 + k], coefs[18 + k], place.sx)
        base = coefs[0]
        out_x = place.ax * trace(base, coefs[9], coefs[18], place.sx)
        upper_y = trace(base, coefs[3], coefs[6], place.sy)
        upper_z = trace_z(base, coefs[1], coefs[2], half)
        wy = place.wy(j)
        wz = place.wz(half)
        kept = (wy * place.sy) * (place.from_y(upper_y) - upper_y) - out_x
        kept = kept + (wz if half else -wz) * (place.from_z(upper_z, half) - upper_z)
        terms = moments(place, j, half, base) + moments(place, j, half, kept) + moments(place, j, half, out_x)
        return tuple(s + t for s, t in zip(sums, terms))

    zero = jnp.zeros((TILE, 128), jnp.float32)
    sums = lax.fori_loop(0, 4, velocity_groups(body), (zero,) * 12)
    sums = [WEIGHT * jnp.sum(s, axis=0, keepdims=True) for s in sums]
    for i, row in enumerate(sums):
        column[pl.ds(i, NZ, stride=COLUMN_ROWS), :] = jnp.broadcast_to(row, (NZ, 128))
    rate_copy.wait()


def between_kernel(column, planes):
    place = Place()
    source = lax.broadcasted_iota(jnp.int32, (NZ, 128), 0)
    source = (source + LEAD) % NZ // 2 + place.vel // (VELS // 2) * (VPD // 2)
    wx = source.astype(jnp.float32) * SPACING + FIRST
    rows = [column[pl.ds(i, NZ, stride=COLUMN_ROWS), :] for i in range(COLUMN_ROWS)]
    held, kept, gone = (all_moments(wx, rows[k : k + 4]) for k in (0, 4, 8))
    for i in range(5):
        planes[pl.ds(i, 4 * BOXES, stride=PLANE_ROWS), :] = jnp.broadcast_to(held[i], (4 * BOXES, 128))
        box = lax.broadcasted_iota(jnp.int32, (4 * BOXES, 128), 0) % BOXES
        sent = jnp.where(box == place.box, kept[i], jnp.where(box == place.downwind, gone[i], 0.0))
        planes[pl.ds(5 + i, 4 * BOXES, stride=PLANE_ROWS), :] = sent


def second_kernel(field, rate, halo, middle, halo_out):
    place = Place()
    collision = jnp.broadcast_to(rate[...], (TILE, 128))

    def body(j, half, start, carry):
        coefs = load_coefs(field, start)
        inflow = [halo[pl.ds(k * COUNT + start, TILE), :] for k in range(9)]
        rates = transport(place, coefs, inflow, j, half)
        new = [c + STEP * (r - collision * c) for c, r in zip(coefs, rates)]
        for m in range(27):
            middle[pl.ds(m * COUNT + start, TILE), :] = new[m]
        for k in range(9):
            halo_out[pl.ds(k * COUNT + start, TILE), :] = trace(new[k], new[9 + k], new[18 + k], place.sx)
        return carry

    lax.fori_loop(0, 4, velocity_groups(body), 0)
    halo_out[FACE - TILE :, :] = collision


def states(totals):
    density = totals[0]
    flow = [t / density for t in totals[1:4]]
    square = flow[0] * flow[0] + flow[1] * flow[1] + flow[2] * flow[2]
    temper = (2.0 * totals[4] / density - square) / 3.0
    spread = 2.0 * math.pi * temper
    return flow, density / (spread * jnp.sqrt(spread)), 0.5 / temper


def maxwell_moments(state):
    flow, scale, inverse = state
    centres = lax.broadcasted_iota(jnp.int32, (16, 128), 0).astype(jnp.float32) * SPACING + FIRST
    sums = []
    for u in flow:
        offset = centres - u
        bell = jnp.exp(-(offset * offset) * inverse)
        sums.append([jnp.sum(v, axis=0, keepdims=True) for v in (bell, centres * bell, centres * centres * bell)])
    (x0, x1, x2), (y0, y1, y2), (z0, z1, z2) = sums
    scale = WEIGHT * scale
    energy = x2 * y0 * z0 + x0 * y2 * z0 + x0 * y0 * z2
    return [
        scale * (x0 * y0 * z0),
        scale * (x1 * y0 * z0),
        scale * (x0 * y1 * z0),
        scale * (x0 * y0 * z1),
        scale * (0.5 * energy),
    ]


def third_kernel(field, rate, halo, planes, middle, out_hbm, out, sems):
    place = Place()

    box = lax.broadcasted_iota(jnp.int32, (4 * BOXES, 128), 0) % BOXES
    rows = [planes[pl.ds(i, 4 * BOXES, stride=PLANE_ROWS), :] for i in range(PLANE_ROWS)]
    total = lambda values: jnp.sum(values, axis=0, keepdims=True)
    totals = [total(jnp.where(box == place.box, r, 0.0)) for r in rows[:5]]
    upwind = [total(jnp.where(box == place.upwind, r, 0.0)) for r in rows[:5]]
    flux = [total(r) for r in rows[5:]]
    nu = rate[...]
    upwind_nu = halo[FACE - 1 :, :]
    now = states(totals)
    gains = maxwell_moments(now)
    later = states([t + STEP * (f - nu * t + nu * g) for t, f, g in zip(totals, flux, gains)])
    before = states(upwind)

    def spread_out(state, factor):
        flow, scale, inverse = state
        wide = lambda v: jnp.broadcast_to(v, (TILE, 128))
        part = (place.wx - flow[0]) * (place.wx - flow[0])
        return wide(part), wide(flow[1]), wide(flow[2]), wide(factor * scale), wide(-inverse)

    now = spread_out(now, STEP * nu)
    before = spread_out(before, STEP * upwind_nu)
    later = spread_out(later, nu)
    collision = jnp.broadcast_to(nu, (TILE, 128))

    def body(j, half, start, carry):
        wy = place.wy(j)
        wz = place.wz(half)

        def bell(state):
            part, flow_y, flow_z, scale, inverse = state
            off_y = wy - flow_y
            off_z = wz - flow_z
            return scale * jnp.exp((part + off_y * off_y + off_z * off_z) * inverse)

        coefs = [middle[pl.ds(m * COUNT + start, TILE), :] for m in range(27)]
        coefs[0] = coefs[0] + bell(now)
        inflow = [halo[pl.ds(k * COUNT + start, TILE), :] for k in range(9)]
        inflow[0] = inflow[0] + bell(before)
        rates = transport(place, coefs, inflow, j, half)
        rates[0] = rates[0] + bell(later)
        for m in range(27):
            here = pl.ds(start * 27 + m, TILE, stride=27)
            moved = coefs[m] + STEP * (rates[m] - collision * coefs[m])
            out[here, :] = 0.5 * field[here, :] + 0.5 * moved
        chunk_copy(out, out_hbm, sems, 2 * j + half, CHUNK // 2).start()
        return carry

    lax.fori_loop(0, 4, velocity_groups(body), 0)
    for j in range(8):
        chunk_copy(out, out_hbm, sems, j, CHUNK // 2).wait()


def call(kernel, outs, *args, remote_in=0, remote_out=False, scratch=()):
    vmem = pl.BlockSpec(memory_space=pltpu.VMEM)
    hbm = pl.BlockSpec(memory_space=pltpu.HBM)
    shapes = [jax.ShapeDtypeStruct(s, jnp.float32) for s in outs]
    moved = sum(4 * math.prod(s) for s in outs) + sum(4 * a.size for a in args)
    return pl.pallas_call(
        kernel,
        out_shape=shapes,
        in_specs=[hbm] * remote_in + [vmem] * (len(args) - remote_in),
        out_specs=[hbm if remote_out else vmem] * len(outs),
        scratch_shapes=scratch,
        compiler_params=pltpu.CompilerParams(vmem_limit_bytes=GRANT),
        cost_estimate=pl.CostEstimate(flops=4000000, bytes_accessed=moved, transcendentals=30000),
    )(*args)


def downwind_pairs():
    pairs = []
    for vel in range(VELS):
        step = 1 if vel >= VELS // 2 else BOXES - 1
        for box in range(BOXES):
            pairs.append((vel * BOXES + box, vel * BOXES + (box + step) % BOXES))
    return pairs


def vel_of(x, z, core):
    return x * 32 + z * 2 + core


PLANES = [
    [vel_of(x, z, core) * BOXES + box for x in range(2) for core in range(2) for box in range(BOXES)]
    for z in range(NZ)
]
COLUMNS = [[vel_of(x, (z + LEAD) % NZ, core) for z in range(NZ)] for x in range(2) for core in range(2)]


def exchange(blocks, axis, groups):
    count = len(groups[0])
    moved = lax.all_to_all(blocks.reshape(count, 1, -1), axis, 0, 0, axis_index_groups=groups)
    return moved.reshape(blocks.shape)


def step(distribution, collision_rate):
    field = pltpu.with_memory_space_constraint(distribution.reshape(COUNT * 27, 128), pltpu.HBM)
    collision_rate = pltpu.with_memory_space_constraint(collision_rate, pltpu.HBM)
    face = (9 * COUNT, 128)
    marked = (FACE, 128)
    whole = (27 * COUNT, 128)
    halo, column, field, rate = call(
        first_kernel,
        [face, (NZ * COLUMN_ROWS, 128), whole, (1, 128)],
        field,
        collision_rate,
        remote_in=2,
        scratch=[pltpu.SemaphoreType.DMA((5,))],
    )
    halo = lax.ppermute(halo, ("vel", "box"), downwind_pairs())
    column = exchange(column, "vel", COLUMNS)
    middle, halo = call(second_kernel, [whole, marked], field, rate, halo)
    halo = lax.ppermute(halo, ("vel", "box"), downwind_pairs())
    (planes,) = call(between_kernel, [(4 * BOXES * PLANE_ROWS, 128)], column)
    planes = exchange(planes, ("vel", "box"), PLANES)
    (out,) = call(
        third_kernel,
        [whole],
        field,
        rate,
        halo,
        planes,
        middle,
        remote_out=True,
        scratch=[pltpu.VMEM(whole, jnp.float32), pltpu.SemaphoreType.DMA((8,))],
    )
    return out.reshape(distribution.shape)


def solution(mesh):
    return jax.shard_map(
        step,
        mesh=mesh,
        in_specs=(P("vel", None, None, None, "box", None), P("box", None)),
        out_specs=P("vel", None, None, None, "box", None),
        check_vma=False,
    )
```

```python
import math

import jax
import jax.numpy as jnp
from jax import lax
from jax.experimental import pallas as pl
from jax.experimental.pallas import tpu as pltpu
from jax.sharding import PartitionSpec as P


NZ = 16
VPD = 16
VELS = 64
LEAD = 9
PLANE_LEAD = 6
BOXES = 8
COUNT = 64
STEP = 0.02
HALF_STEP = 0.5 * STEP
SPACING = 0.5
FIRST = -3.75
WEIGHT = SPACING**3
COLUMN_ROWS = 12
PLANE_ROWS = 10
TILE = 8
GRANT = 16 << 20
CHUNK = COUNT * 27 // 4
FACE = 9 * COUNT + TILE


def mode(a, b, c):
    return 9 * a + 3 * b + c


def row_index():
    return lax.broadcasted_iota(jnp.int32, (TILE, 128), 0)


class Place:
    def __init__(self):
        self.vel = lax.axis_index("vel")
        self.box = lax.axis_index("box")
        right = self.vel >= VELS // 2
        self.sx = jnp.where(right, 1.0, -1.0)
        self.wx = (self.vel // 4).astype(jnp.float32) * SPACING + FIRST
        self.ax = self.wx * self.sx
        up = self.vel % 4 >= 2
        self.sy = jnp.where(up, 1.0, -1.0)
        self.first_y = (self.vel % 4 * 4).astype(jnp.float32) * SPACING + FIRST
        self.shift_y = jnp.where(up, NZ, 128 - NZ)
        self.upwind = jnp.where(right, (self.box + BOXES - 1) % BOXES, (self.box + 1) % BOXES)
        self.downwind = jnp.where(right, (self.box + 1) % BOXES, (self.box + BOXES - 1) % BOXES)
        self.lane = lax.broadcasted_iota(jnp.int32, (TILE, 128), 1) % NZ

    def wy(self, j):
        return self.first_y + j.astype(jnp.float32) * SPACING

    def wz(self, half):
        return row_index().astype(jnp.float32) * SPACING + (FIRST + half * TILE * SPACING)

    def from_y(self, values):
        return pltpu.roll(values, self.shift_y, 1)

    def from_z(self, values, half):
        if half:
            return jnp.where(self.lane == 0, pltpu.roll(values, 128 + 1 - NZ, 1), pltpu.roll(values, 1, 1))
        return jnp.where(self.lane == NZ - 1, pltpu.roll(values, NZ - 1, 1), pltpu.roll(values, 127, 1))


def trace(low, middle, high, sign):
    return low + sign * middle + high


def trace_z(low, middle, high, half):
    return low + middle + high if half else low - middle + high


def one_direction(rates, coefs, index, upper, inflow, speed, size):
    _, i1, i2 = index
    jump = -upper if inflow is None else inflow - upper
    parts = (
        size * jump,
        (-3.0 * speed) * jump - (6.0 * size) * coefs[i1] - (6.0 * speed) * coefs[i2],
        (5.0 * size) * jump + (10.0 * speed) * coefs[i1],
    )
    for i, part in zip(index, parts):
        rates[i] = part if rates[i] is None else rates[i] + part


def transport(place, coefs, inflow_x, j, half):
    rates = [None] * 27
    for b in range(3):
        for c in range(3):
            index = [mode(a, b, c) for a in range(3)]
            upper = trace(*(coefs[i] for i in index), place.sx)
            one_direction(rates, coefs, index, upper, inflow_x and inflow_x[3 * b + c], place.wx, place.ax)
    wy = place.wy(j)
    ay = wy * place.sy
    for a in range(3):
        for c in range(3):
            index = [mode(a, b, c) for b in range(3)]
            upper = trace(*(coefs[i] for i in index), place.sy)
            one_direction(rates, coefs, index, upper, place.from_y(upper), wy, ay)
    wz = place.wz(half)
    az = wz if half else -wz
    for a in range(3):
        for b in range(3):
            index = [mode(a, b, c) for c in range(3)]
            upper = trace_z(*(coefs[i] for i in index), half)
            one_direction(rates, coefs, index, upper, place.from_z(upper, half), wz, az)
    return rates


def velocity_groups(body):
    def step(j, carry):
        for half in range(2):
            carry = body(j, half, pl.multiple_of((2 * j + half) * TILE, TILE), carry)
        return carry

    return step


def load_coefs(field, start):
    return [field[pl.ds(start * 27 + m, TILE, stride=27), :] for m in range(27)]


def moments(place, j, half, values):
    wy = place.wy(j)
    wz = place.wz(half)
    return [values, wy * values, wz * values, (0.5 * (wy * wy + wz * wz)) * values]


def all_moments(wx, four):
    total = lambda values: jnp.sum(values, axis=0, keepdims=True)
    count, along_y, along_z, energy = four
    return [
        total(count),
        total(wx * count),
        total(along_y),
        total(along_z),
        total(energy + (0.5 * (wx * wx)) * count),
    ]


def chunk_copy(source, target, sems, j, size=CHUNK):
    rows = pl.ds(pl.multiple_of(j * size, size), size)
    return pltpu.make_async_copy(source.at[rows], target.at[rows], sems.at[j])


def first_kernel(field_hbm, rate_hbm, halo, column_hbm, field, rate, column, sems):
    place = Place()
    for j in range(4):
        chunk_copy(field_hbm, field, sems, j).start()
    rate_copy = pltpu.make_async_copy(rate_hbm, rate, sems.at[4])
    rate_copy.start()

    def sums_of(j, half, start, sums):
        if not half:
            chunk_copy(field_hbm, field, sems, j).wait()
        base, x1, x2, y1, y2, z1, z2 = (
            field[pl.ds(start * 27 + m, TILE, stride=27), :] for m in (0, 9, 18, 3, 6, 1, 2)
        )
        out_x = place.ax * trace(base, x1, x2, place.sx)
        upper_y = trace(base, y1, y2, place.sy)
        upper_z = trace_z(base, z1, z2, half)
        wy = place.wy(j)
        wz = place.wz(half)
        kept = (wy * place.sy) * (place.from_y(upper_y) - upper_y) - out_x
        kept = kept + (wz if half else -wz) * (place.from_z(upper_z, half) - upper_z)
        terms = moments(place, j, half, base) + moments(place, j, half, kept) + moments(place, j, half, out_x)
        return tuple(s + t for s, t in zip(sums, terms))

    zero = jnp.zeros((TILE, 128), jnp.float32)
    sums = lax.fori_loop(0, 4, velocity_groups(sums_of), (zero,) * 12)
    for i, s in enumerate(sums):
        row = WEIGHT * jnp.sum(s, axis=0, keepdims=True)
        column[pl.ds(i, NZ, stride=COLUMN_ROWS), :] = jnp.broadcast_to(row, (NZ, 128))
    column_copy = pltpu.make_async_copy(column, column_hbm, sems.at[5])
    column_copy.start()

    def traces_of(j, half, start, carry):
        coefs = load_coefs(field, start)
        for k in range(9):
            halo[pl.ds(k * COUNT + start, TILE), :] = trace(coefs[k], coefs[9 + k], coefs[18 + k], place.sx)
        return carry

    lax.fori_loop(0, 4, velocity_groups(traces_of), 0)
    rate_copy.wait()
    column_copy.wait()


def between_kernel(column, planes):
    place = Place()
    source = lax.broadcasted_iota(jnp.int32, (NZ, 128), 0)
    source = (source + LEAD) % NZ // 2 + place.vel // (VELS // 2) * (VPD // 2)
    wx = source.astype(jnp.float32) * SPACING + FIRST
    rows = [column[pl.ds(i, NZ, stride=COLUMN_ROWS), :] for i in range(COLUMN_ROWS)]
    held, kept, gone = (all_moments(wx, rows[k : k + 4]) for k in (0, 4, 8))
    for i in range(5):
        planes[pl.ds(i, 4 * BOXES, stride=PLANE_ROWS), :] = jnp.broadcast_to(held[i], (4 * BOXES, 128))
        box = (lax.broadcasted_iota(jnp.int32, (4 * BOXES, 128), 0) + PLANE_LEAD) % BOXES
        sent = jnp.where(box == place.box, kept[i], jnp.where(box == place.downwind, gone[i], 0.0))
        planes[pl.ds(5 + i, 4 * BOXES, stride=PLANE_ROWS), :] = sent


def second_kernel(field, rate, halo, middle, halo_out):
    place = Place()
    collision = jnp.broadcast_to(rate[...], (TILE, 128))

    def body(j, half, start, carry):
        coefs = load_coefs(field, start)
        inflow = [halo[pl.ds(k * COUNT + start, TILE), :] for k in range(9)]
        rates = transport(place, coefs, inflow, j, half)
        new = [c + STEP * (r - collision * c) for c, r in zip(coefs, rates)]
        for m in range(27):
            middle[pl.ds(m * COUNT + start, TILE), :] = new[m]
        for k in range(9):
            halo_out[pl.ds(k * COUNT + start, TILE), :] = trace(new[k], new[9 + k], new[18 + k], place.sx)
        return carry

    lax.fori_loop(0, 4, velocity_groups(body), 0)
    halo_out[FACE - TILE :, :] = collision


def base_kernel(field, rate, middle, base):
    place = Place()
    collision = jnp.broadcast_to(rate[...], (TILE, 128))

    def body(j, half, start, carry):
        coefs = [middle[pl.ds(m * COUNT + start, TILE), :] for m in range(27)]
        rates = transport(place, coefs, None, j, half)
        for m in range(27):
            moved = coefs[m] + STEP * (rates[m] - collision * coefs[m])
            old = field[pl.ds(start * 27 + m, TILE, stride=27), :]
            base[pl.ds(m * COUNT + start, TILE), :] = 0.5 * old + 0.5 * moved
        return carry

    lax.fori_loop(0, 4, velocity_groups(body), 0)


def states(totals):
    density = totals[0]
    flow = [t / density for t in totals[1:4]]
    square = flow[0] * flow[0] + flow[1] * flow[1] + flow[2] * flow[2]
    temper = (2.0 * totals[4] / density - square) / 3.0
    spread = 2.0 * math.pi * temper
    return flow, density / (spread * jnp.sqrt(spread)), 0.5 / temper


def maxwell_moments(state):
    flow, scale, inverse = state
    centres = lax.broadcasted_iota(jnp.int32, (16, 128), 0).astype(jnp.float32) * SPACING + FIRST
    sums = []
    for u in flow:
        offset = centres - u
        bell = jnp.exp(-(offset * offset) * inverse)
        sums.append([jnp.sum(v, axis=0, keepdims=True) for v in (bell, centres * bell, centres * centres * bell)])
    (x0, x1, x2), (y0, y1, y2), (z0, z1, z2) = sums
    scale = WEIGHT * scale
    energy = x2 * y0 * z0 + x0 * y2 * z0 + x0 * y0 * z2
    return [
        scale * (x0 * y0 * z0),
        scale * (x1 * y0 * z0),
        scale * (x0 * y1 * z0),
        scale * (x0 * y0 * z1),
        scale * (0.5 * energy),
    ]


def third_kernel(rate, halo, planes, base, out_hbm, out, sems):
    place = Place()

    box = (lax.broadcasted_iota(jnp.int32, (4 * BOXES, 128), 0) + PLANE_LEAD) % BOXES
    rows = [planes[pl.ds(i, 4 * BOXES, stride=PLANE_ROWS), :] for i in range(PLANE_ROWS)]
    total = lambda values: jnp.sum(values, axis=0, keepdims=True)
    totals = [total(jnp.where(box == place.box, r, 0.0)) for r in rows[:5]]
    upwind = [total(jnp.where(box == place.upwind, r, 0.0)) for r in rows[:5]]
    flux = [total(r) for r in rows[5:]]
    nu = rate[...]
    upwind_nu = halo[FACE - 1 :, :]
    now = states(totals)
    gains = maxwell_moments(now)
    later = states([t + STEP * (f - nu * t + nu * g) for t, f, g in zip(totals, flux, gains)])
    before = states(upwind)

    def spread_out(state, factor):
        flow, scale, inverse = state
        wide = lambda v: jnp.broadcast_to(v, (TILE, 128))
        part = (place.wx - flow[0]) * (place.wx - flow[0])
        return wide(part), wide(flow[1]), wide(flow[2]), wide(factor * scale), wide(-inverse)

    now = spread_out(now, STEP * nu)
    before = spread_out(before, STEP * upwind_nu)
    later = spread_out(later, HALF_STEP * nu)
    gain = HALF_STEP * place.ax
    speed = HALF_STEP * place.wx
    collision = jnp.broadcast_to(nu, (TILE, 128))

    def body(j, half, start, carry):
        wy = place.wy(j)
        wz = place.wz(half)

        def bell(state):
            part, flow_y, flow_z, scale, inverse = state
            off_y = wy - flow_y
            off_z = wz - flow_z
            return scale * jnp.exp((part + off_y * off_y + off_z * off_z) * inverse)

        added = [None] * 27
        extra = bell(now)
        inflow = [halo[pl.ds(k * COUNT + start, TILE), :] for k in range(9)]
        inflow[0] = inflow[0] + bell(before) - extra
        for k in range(9):
            added[k] = gain * inflow[k]
            added[9 + k] = (-3.0 * speed) * inflow[k]
            added[18 + k] = (5.0 * gain) * inflow[k]
        added[0] = added[0] + (0.5 - HALF_STEP * collision) * extra + bell(later)
        lines = (
            (HALF_STEP * wy, HALF_STEP * (wy * place.sy), place.from_y(extra) - extra, 3),
            (HALF_STEP * wz, HALF_STEP * (wz if half else -wz), place.from_z(extra, half) - extra, 1),
        )
        for line, size, jump, i in lines:
            added[0] = added[0] + size * jump
            added[i] = added[i] - (3.0 * line) * jump
            added[2 * i] = added[2 * i] + (5.0 * size) * jump
        for m in range(27):
            out[pl.ds(start * 27 + m, TILE, stride=27), :] = base[pl.ds(m * COUNT + start, TILE), :] + added[m]
        chunk_copy(out, out_hbm, sems, 2 * j + half, CHUNK // 2).start()
        return carry

    lax.fori_loop(0, 4, velocity_groups(body), 0)
    for j in range(8):
        chunk_copy(out, out_hbm, sems, j, CHUNK // 2).wait()


def call(kernel, outs, *args, remote_in=0, remote_out=(), scratch=()):
    vmem = pl.BlockSpec(memory_space=pltpu.VMEM)
    hbm = pl.BlockSpec(memory_space=pltpu.HBM)
    shapes = [jax.ShapeDtypeStruct(s, jnp.float32) for s in outs]
    moved = sum(4 * math.prod(s) for s in outs) + sum(4 * a.size for a in args)
    return pl.pallas_call(
        kernel,
        out_shape=shapes,
        in_specs=[hbm] * remote_in + [vmem] * (len(args) - remote_in),
        out_specs=[hbm if i in remote_out else vmem for i in range(len(outs))],
        scratch_shapes=scratch,
        compiler_params=pltpu.CompilerParams(vmem_limit_bytes=GRANT),
        cost_estimate=pl.CostEstimate(flops=4000000, bytes_accessed=moved, transcendentals=30000),
    )(*args)


def downwind_pairs():
    pairs = []
    for vel in range(VELS):
        step = 1 if vel >= VELS // 2 else BOXES - 1
        for box in range(BOXES):
            pairs.append((vel * BOXES + box, vel * BOXES + (box + step) % BOXES))
    return pairs


def vel_of(x, z, core):
    return x * 32 + z * 2 + core


PLANES = [
    [vel_of(x, z, core) * BOXES + box for x in range(2) for core in range(2) for box in range(BOXES)]
    for z in range(NZ)
]
PLANES = [group[PLANE_LEAD:] + group[:PLANE_LEAD] for group in PLANES]
COLUMNS = [[vel_of(x, (z + LEAD) % NZ, core) for z in range(NZ)] for x in range(2) for core in range(2)]


def exchange(blocks, axis, groups):
    count = len(groups[0])
    moved = lax.all_to_all(blocks.reshape(count, 1, -1), axis, 0, 0, axis_index_groups=groups)
    return moved.reshape(blocks.shape)


def step(distribution, collision_rate):
    field = pltpu.with_memory_space_constraint(distribution.reshape(COUNT * 27, 128), pltpu.HBM)
    collision_rate = pltpu.with_memory_space_constraint(collision_rate, pltpu.HBM)
    face = (9 * COUNT, 128)
    marked = (FACE, 128)
    whole = (27 * COUNT, 128)
    halo, column, field, rate = call(
        first_kernel,
        [face, (NZ * COLUMN_ROWS, 128), whole, (1, 128)],
        field,
        collision_rate,
        remote_in=2,
        remote_out=(1,),
        scratch=[pltpu.VMEM((NZ * COLUMN_ROWS, 128), jnp.float32), pltpu.SemaphoreType.DMA((6,))],
    )
    halo = lax.ppermute(halo, ("vel", "box"), downwind_pairs())
    column = exchange(column, "vel", COLUMNS)
    middle, halo = call(second_kernel, [whole, marked], field, rate, halo)
    halo = lax.ppermute(halo, ("vel", "box"), downwind_pairs())
    (base,) = call(base_kernel, [whole], field, rate, middle)
    (planes,) = call(between_kernel, [(4 * BOXES * PLANE_ROWS, 128)], column)
    planes = exchange(planes, ("vel", "box"), PLANES)
    (out,) = call(
        third_kernel,
        [whole],
        rate,
        halo,
        planes,
        base,
        remote_out=(0,),
        scratch=[pltpu.VMEM(whole, jnp.float32), pltpu.SemaphoreType.DMA((8,))],
    )
    return out.reshape(distribution.shape)


def solution(mesh):
    return jax.shard_map(
        step,
        mesh=mesh,
        in_specs=(P("vel", None, None, None, "box", None), P("box", None)),
        out_specs=P("vel", None, None, None, "box", None),
        check_vma=False,
    )
```

```python
import math

import jax
import jax.numpy as jnp
from jax import lax
from jax.experimental import pallas as pl
from jax.experimental.pallas import tpu as pltpu
from jax.sharding import PartitionSpec as P


NZ = 16
VPD = 16
VELS = 64
LEAD = 10
PLANE_LEAD = 14
BOXES = 8
COUNT = 64
STEP = 0.02
HALF_STEP = 0.5 * STEP
SPACING = 0.5
FIRST = -3.75
WEIGHT = SPACING**3
COLUMN_ROWS = 12
PLANE_ROWS = 10
TILE = 8
GRANT = 16 << 20
CHUNK = COUNT * 27 // 4
FACE = 9 * COUNT + TILE


def mode(a, b, c):
    return 9 * a + 3 * b + c


def row_index():
    return lax.broadcasted_iota(jnp.int32, (TILE, 128), 0)


class Place:
    def __init__(self):
        self.vel = lax.axis_index("vel")
        self.box = lax.axis_index("box")
        right = self.vel >= VELS // 2
        self.sx = jnp.where(right, 1.0, -1.0)
        self.wx = (self.vel // 4).astype(jnp.float32) * SPACING + FIRST
        self.ax = self.wx * self.sx
        up = self.vel % 4 >= 2
        self.sy = jnp.where(up, 1.0, -1.0)
        self.first_y = (self.vel % 4 * 4).astype(jnp.float32) * SPACING + FIRST
        self.shift_y = jnp.where(up, NZ, 128 - NZ)
        self.upwind = jnp.where(right, (self.box + BOXES - 1) % BOXES, (self.box + 1) % BOXES)
        self.downwind = jnp.where(right, (self.box + 1) % BOXES, (self.box + BOXES - 1) % BOXES)
        self.waits = jnp.logical_not(right) & (self.box % (BOXES // 2) == 0)
        self.lane = lax.broadcasted_iota(jnp.int32, (TILE, 128), 1) % NZ

    def wy(self, j):
        return self.first_y + j.astype(jnp.float32) * SPACING

    def wz(self, half):
        return row_index().astype(jnp.float32) * SPACING + (FIRST + half * TILE * SPACING)

    def from_y(self, values):
        return pltpu.roll(values, self.shift_y, 1)

    def from_z(self, values, half):
        if half:
            return jnp.where(self.lane == 0, pltpu.roll(values, 128 + 1 - NZ, 1), pltpu.roll(values, 1, 1))
        return jnp.where(self.lane == NZ - 1, pltpu.roll(values, NZ - 1, 1), pltpu.roll(values, 127, 1))


def trace(low, middle, high, sign):
    return low + sign * middle + high


def trace_z(low, middle, high, half):
    return low + middle + high if half else low - middle + high


def one_direction(rates, coefs, index, upper, inflow, speed, size):
    _, i1, i2 = index
    jump = -upper if inflow is None else inflow - upper
    parts = (
        size * jump,
        (-3.0 * speed) * jump - (6.0 * size) * coefs[i1] - (6.0 * speed) * coefs[i2],
        (5.0 * size) * jump + (10.0 * speed) * coefs[i1],
    )
    for i, part in zip(index, parts):
        rates[i] = part if rates[i] is None else rates[i] + part


def transport(place, coefs, inflow_x, j, half):
    rates = [None] * 27
    for b in range(3):
        for c in range(3):
            index = [mode(a, b, c) for a in range(3)]
            upper = trace(*(coefs[i] for i in index), place.sx)
            one_direction(rates, coefs, index, upper, inflow_x and inflow_x[3 * b + c], place.wx, place.ax)
    wy = place.wy(j)
    ay = wy * place.sy
    for a in range(3):
        for c in range(3):
            index = [mode(a, b, c) for b in range(3)]
            upper = trace(*(coefs[i] for i in index), place.sy)
            one_direction(rates, coefs, index, upper, place.from_y(upper), wy, ay)
    wz = place.wz(half)
    az = wz if half else -wz
    for a in range(3):
        for b in range(3):
            index = [mode(a, b, c) for c in range(3)]
            upper = trace_z(*(coefs[i] for i in index), half)
            one_direction(rates, coefs, index, upper, place.from_z(upper, half), wz, az)
    return rates


def velocity_groups(body):
    def step(j, carry):
        for half in range(2):
            carry = body(j, half, pl.multiple_of((2 * j + half) * TILE, TILE), carry)
        return carry

    return step


def load_coefs(field, start):
    return [field[pl.ds(start * 27 + m, TILE, stride=27), :] for m in range(27)]


def moments(place, j, half, values):
    wy = place.wy(j)
    wz = place.wz(half)
    return [values, wy * values, wz * values, (0.5 * (wy * wy + wz * wz)) * values]


def all_moments(wx, four):
    total = lambda values: jnp.sum(values, axis=0, keepdims=True)
    count, along_y, along_z, energy = four
    return [
        total(count),
        total(wx * count),
        total(along_y),
        total(along_z),
        total(energy + (0.5 * (wx * wx)) * count),
    ]


def chunk_copy(source, target, sems, j, size=CHUNK):
    rows = pl.ds(pl.multiple_of(j * size, size), size)
    return pltpu.make_async_copy(source.at[rows], target.at[rows], sems.at[j])


def send_moments(place, field, column, column_hbm, sem):
    def sums_of(j, half, start, sums):
        base, x1, x2, y1, y2, z1, z2 = (
            field[pl.ds(start * 27 + m, TILE, stride=27), :] for m in (0, 9, 18, 3, 6, 1, 2)
        )
        out_x = place.ax * trace(base, x1, x2, place.sx)
        upper_y = trace(base, y1, y2, place.sy)
        upper_z = trace_z(base, z1, z2, half)
        wy = place.wy(j)
        wz = place.wz(half)
        kept = (wy * place.sy) * (place.from_y(upper_y) - upper_y) - out_x
        kept = kept + (wz if half else -wz) * (place.from_z(upper_z, half) - upper_z)
        terms = moments(place, j, half, base) + moments(place, j, half, kept) + moments(place, j, half, out_x)
        return tuple(s + t for s, t in zip(sums, terms))

    zero = jnp.zeros((TILE, 128), jnp.float32)
    sums = lax.fori_loop(0, 4, velocity_groups(sums_of), (zero,) * 12)
    for i, s in enumerate(sums):
        row = WEIGHT * jnp.sum(s, axis=0, keepdims=True)
        column[pl.ds(i, NZ, stride=COLUMN_ROWS), :] = jnp.broadcast_to(row, (NZ, 128))
    copy = pltpu.make_async_copy(column, column_hbm, sem)
    copy.start()
    copy.wait()


def first_kernel(field_hbm, rate_hbm, halo, column_hbm, field, rate, column, sems):
    place = Place()
    for j in range(4):
        chunk_copy(field_hbm, field, sems, j).start()
    rate_copy = pltpu.make_async_copy(rate_hbm, rate, sems.at[4])
    rate_copy.start()

    def traces_of(j, half, start, carry):
        if not half:
            chunk_copy(field_hbm, field, sems, j).wait()
        coefs = load_coefs(field, start)
        for k in range(9):
            halo[pl.ds(k * COUNT + start, TILE), :] = trace(coefs[k], coefs[9 + k], coefs[18 + k], place.sx)
        return carry

    lax.fori_loop(0, 4, velocity_groups(traces_of), 0)
    rate_copy.wait()

    @pl.when(place.waits)
    def _():
        send_moments(place, field, column, column_hbm, sems.at[5])


def moments_kernel(field, _, column_hbm, column, sems):
    place = Place()

    @pl.when(jnp.logical_not(place.waits))
    def _():
        send_moments(place, field, column, column_hbm, sems.at[0])


def between_kernel(column, planes):
    place = Place()
    source = lax.broadcasted_iota(jnp.int32, (NZ, 128), 0)
    source = (source + LEAD) % NZ // 2 + place.vel // (VELS // 2) * (VPD // 2)
    wx = source.astype(jnp.float32) * SPACING + FIRST
    rows = [column[pl.ds(i, NZ, stride=COLUMN_ROWS), :] for i in range(COLUMN_ROWS)]
    held, kept, gone = (all_moments(wx, rows[k : k + 4]) for k in (0, 4, 8))
    for i in range(5):
        planes[pl.ds(i, 4 * BOXES, stride=PLANE_ROWS), :] = jnp.broadcast_to(held[i], (4 * BOXES, 128))
        box = (lax.broadcasted_iota(jnp.int32, (4 * BOXES, 128), 0) + PLANE_LEAD) % BOXES
        sent = jnp.where(box == place.box, kept[i], jnp.where(box == place.downwind, gone[i], 0.0))
        planes[pl.ds(5 + i, 4 * BOXES, stride=PLANE_ROWS), :] = sent


def second_kernel(field, rate, halo, middle, halo_out):
    place = Place()
    collision = jnp.broadcast_to(rate[...], (TILE, 128))

    def body(j, half, start, carry):
        coefs = load_coefs(field, start)
        inflow = [halo[pl.ds(k * COUNT + start, TILE), :] for k in range(9)]
        rates = transport(place, coefs, inflow, j, half)
        new = [c + STEP * (r - collision * c) for c, r in zip(coefs, rates)]
        for m in range(27):
            middle[pl.ds(m * COUNT + start, TILE), :] = new[m]
        for k in range(9):
            halo_out[pl.ds(k * COUNT + start, TILE), :] = trace(new[k], new[9 + k], new[18 + k], place.sx)
        return carry

    lax.fori_loop(0, 4, velocity_groups(body), 0)
    halo_out[FACE - TILE :, :] = collision


def base_kernel(field, rate, middle, base):
    place = Place()
    collision = jnp.broadcast_to(rate[...], (TILE, 128))

    def body(j, half, start, carry):
        coefs = [middle[pl.ds(m * COUNT + start, TILE), :] for m in range(27)]
        rates = transport(place, coefs, None, j, half)
        for m in range(27):
            moved = coefs[m] + STEP * (rates[m] - collision * coefs[m])
            old = field[pl.ds(start * 27 + m, TILE, stride=27), :]
            base[pl.ds(m * COUNT + start, TILE), :] = 0.5 * old + 0.5 * moved
        return carry

    lax.fori_loop(0, 4, velocity_groups(body), 0)


def states(totals):
    density = totals[0]
    flow = [t / density for t in totals[1:4]]
    square = flow[0] * flow[0] + flow[1] * flow[1] + flow[2] * flow[2]
    temper = (2.0 * totals[4] / density - square) / 3.0
    spread = 2.0 * math.pi * temper
    return flow, density / (spread * jnp.sqrt(spread)), 0.5 / temper


def maxwell_moments(state):
    flow, scale, inverse = state
    centres = lax.broadcasted_iota(jnp.int32, (16, 128), 0).astype(jnp.float32) * SPACING + FIRST
    sums = []
    for u in flow:
        offset = centres - u
        bell = jnp.exp(-(offset * offset) * inverse)
        sums.append([jnp.sum(v, axis=0, keepdims=True) for v in (bell, centres * bell, centres * centres * bell)])
    (x0, x1, x2), (y0, y1, y2), (z0, z1, z2) = sums
    scale = WEIGHT * scale
    energy = x2 * y0 * z0 + x0 * y2 * z0 + x0 * y0 * z2
    return [
        scale * (x0 * y0 * z0),
        scale * (x1 * y0 * z0),
        scale * (x0 * y1 * z0),
        scale * (x0 * y0 * z1),
        scale * (0.5 * energy),
    ]


def third_kernel(rate, halo, planes, base, out_hbm, out, sems):
    place = Place()

    box = (lax.broadcasted_iota(jnp.int32, (4 * BOXES, 128), 0) + PLANE_LEAD) % BOXES
    rows = [planes[pl.ds(i, 4 * BOXES, stride=PLANE_ROWS), :] for i in range(PLANE_ROWS)]
    total = lambda values: jnp.sum(values, axis=0, keepdims=True)
    totals = [total(jnp.where(box == place.box, r, 0.0)) for r in rows[:5]]
    upwind = [total(jnp.where(box == place.upwind, r, 0.0)) for r in rows[:5]]
    flux = [total(r) for r in rows[5:]]
    nu = rate[...]
    upwind_nu = halo[FACE - 1 :, :]
    now = states(totals)
    gains = maxwell_moments(now)
    later = states([t + STEP * (f - nu * t + nu * g) for t, f, g in zip(totals, flux, gains)])
    before = states(upwind)

    def spread_out(state, factor):
        flow, scale, inverse = state
        wide = lambda v: jnp.broadcast_to(v, (TILE, 128))
        part = (place.wx - flow[0]) * (place.wx - flow[0])
        return wide(part), wide(flow[1]), wide(flow[2]), wide(factor * scale), wide(-inverse)

    now = spread_out(now, STEP * nu)
    before = spread_out(before, STEP * upwind_nu)
    later = spread_out(later, HALF_STEP * nu)
    gain = HALF_STEP * place.ax
    speed = HALF_STEP * place.wx
    collision = jnp.broadcast_to(nu, (TILE, 128))

    def body(j, half, start, carry):
        wy = place.wy(j)
        wz = place.wz(half)

        def bell(state):
            part, flow_y, flow_z, scale, inverse = state
            off_y = wy - flow_y
            off_z = wz - flow_z
            return scale * jnp.exp((part + off_y * off_y + off_z * off_z) * inverse)

        added = [None] * 27
        extra = bell(now)
        inflow = [halo[pl.ds(k * COUNT + start, TILE), :] for k in range(9)]
        inflow[0] = inflow[0] + bell(before) - extra
        for k in range(9):
            added[k] = gain * inflow[k]
            added[9 + k] = (-3.0 * speed) * inflow[k]
            added[18 + k] = (5.0 * gain) * inflow[k]
        added[0] = added[0] + (0.5 - HALF_STEP * collision) * extra + bell(later)
        lines = (
            (HALF_STEP * wy, HALF_STEP * (wy * place.sy), place.from_y(extra) - extra, 3),
            (HALF_STEP * wz, HALF_STEP * (wz if half else -wz), place.from_z(extra, half) - extra, 1),
        )
        for line, size, jump, i in lines:
            added[0] = added[0] + size * jump
            added[i] = added[i] - (3.0 * line) * jump
            added[2 * i] = added[2 * i] + (5.0 * size) * jump
        for m in range(27):
            out[pl.ds(start * 27 + m, TILE, stride=27), :] = base[pl.ds(m * COUNT + start, TILE), :] + added[m]
        chunk_copy(out, out_hbm, sems, 2 * j + half, CHUNK // 2).start()
        return carry

    lax.fori_loop(0, 4, velocity_groups(body), 0)
    for j in range(8):
        chunk_copy(out, out_hbm, sems, j, CHUNK // 2).wait()


def call(kernel, outs, *args, remote_in=(), remote_out=(), scratch=(), aliases=None):
    vmem = pl.BlockSpec(memory_space=pltpu.VMEM)
    hbm = pl.BlockSpec(memory_space=pltpu.HBM)
    shapes = [jax.ShapeDtypeStruct(s, jnp.float32) for s in outs]
    moved = sum(4 * math.prod(s) for s in outs) + sum(4 * a.size for a in args)
    return pl.pallas_call(
        kernel,
        out_shape=shapes,
        in_specs=[hbm if i in remote_in else vmem for i in range(len(args))],
        out_specs=[hbm if i in remote_out else vmem for i in range(len(outs))],
        scratch_shapes=scratch,
        input_output_aliases=aliases or {},
        compiler_params=pltpu.CompilerParams(vmem_limit_bytes=GRANT),
        cost_estimate=pl.CostEstimate(flops=4000000, bytes_accessed=moved, transcendentals=30000),
    )(*args)


def downwind_pairs():
    pairs = []
    for vel in range(VELS):
        step = 1 if vel >= VELS // 2 else BOXES - 1
        for box in range(BOXES):
            pairs.append((vel * BOXES + box, vel * BOXES + (box + step) % BOXES))
    return pairs


def vel_of(x, z, core):
    return x * 32 + z * 2 + core


PLANES = [
    [vel_of(x, z, core) * BOXES + box for x in range(2) for core in range(2) for box in range(BOXES)]
    for z in range(NZ)
]
PLANES = [group[PLANE_LEAD:] + group[:PLANE_LEAD] for group in PLANES]
COLUMNS = [[vel_of(x, (z + LEAD) % NZ, core) for z in range(NZ)] for x in range(2) for core in range(2)]


def exchange(blocks, axis, groups):
    count = len(groups[0])
    moved = lax.all_to_all(blocks.reshape(count, 1, -1), axis, 0, 0, axis_index_groups=groups)
    return moved.reshape(blocks.shape)


def step(distribution, collision_rate):
    field = pltpu.with_memory_space_constraint(distribution.reshape(COUNT * 27, 128), pltpu.HBM)
    collision_rate = pltpu.with_memory_space_constraint(collision_rate, pltpu.HBM)
    face = (9 * COUNT, 128)
    marked = (FACE, 128)
    whole = (27 * COUNT, 128)
    halo, column, field, rate = call(
        first_kernel,
        [face, (NZ * COLUMN_ROWS, 128), whole, (1, 128)],
        field,
        collision_rate,
        remote_in=(0, 1),
        remote_out=(1,),
        scratch=[pltpu.VMEM((NZ * COLUMN_ROWS, 128), jnp.float32), pltpu.SemaphoreType.DMA((6,))],
    )
    halo = lax.ppermute(halo, ("vel", "box"), downwind_pairs())
    (column,) = call(
        moments_kernel,
        [(NZ * COLUMN_ROWS, 128)],
        field,
        column,
        remote_in=(1,),
        remote_out=(0,),
        scratch=[pltpu.VMEM((NZ * COLUMN_ROWS, 128), jnp.float32), pltpu.SemaphoreType.DMA((1,))],
        aliases={1: 0},
    )
    column = exchange(column, "vel", COLUMNS)
    middle, halo = call(second_kernel, [whole, marked], field, rate, halo)
    halo = lax.ppermute(halo, ("vel", "box"), downwind_pairs())
    (base,) = call(base_kernel, [whole], field, rate, middle)
    (planes,) = call(between_kernel, [(4 * BOXES * PLANE_ROWS, 128)], column)
    planes = exchange(planes, ("vel", "box"), PLANES)
    (out,) = call(
        third_kernel,
        [whole],
        rate,
        halo,
        planes,
        base,
        remote_out=(0,),
        scratch=[pltpu.VMEM(whole, jnp.float32), pltpu.SemaphoreType.DMA((8,))],
    )
    return out.reshape(distribution.shape)


def solution(mesh):
    return jax.shard_map(
        step,
        mesh=mesh,
        in_specs=(P("vel", None, None, None, "box", None), P("box", None)),
        out_specs=P("vel", None, None, None, "box", None),
        check_vma=False,
    )
```

```python
import math

import jax
import jax.numpy as jnp
from jax import lax
from jax.experimental import pallas as pl
from jax.experimental.pallas import tpu as pltpu
from jax.sharding import PartitionSpec as P


NZ = 16
VPD = 16
VELS = 64
LEAD = 10
PLANE_LEAD = 14
BOXES = 8
COUNT = 64
STEP = 0.02
HALF_STEP = 0.5 * STEP
SPACING = 0.5
FIRST = -3.75
WEIGHT = SPACING**3
COLUMN_ROWS = 12
PLANE_ROWS = 10
TILE = 8
GRANT = 16 << 20
CHUNK = COUNT * 27 // 4
FACE = 9 * COUNT + TILE


def mode(a, b, c):
    return 9 * a + 3 * b + c


def row_index():
    return lax.broadcasted_iota(jnp.int32, (TILE, 128), 0)


class Place:
    def __init__(self):
        self.vel = lax.axis_index("vel")
        self.box = lax.axis_index("box")
        right = self.vel >= VELS // 2
        self.sx = jnp.where(right, 1.0, -1.0)
        self.wx = (self.vel // 4).astype(jnp.float32) * SPACING + FIRST
        self.ax = self.wx * self.sx
        up = self.vel % 4 >= 2
        self.sy = jnp.where(up, 1.0, -1.0)
        self.first_y = (self.vel % 4 * 4).astype(jnp.float32) * SPACING + FIRST
        self.shift_y = jnp.where(up, NZ, 128 - NZ)
        self.upwind = jnp.where(right, (self.box + BOXES - 1) % BOXES, (self.box + 1) % BOXES)
        self.downwind = jnp.where(right, (self.box + 1) % BOXES, (self.box + BOXES - 1) % BOXES)
        self.waits = jnp.logical_not(right) & (self.box % (BOXES // 2) == 0)
        self.lane = lax.broadcasted_iota(jnp.int32, (TILE, 128), 1) % NZ

    def wy(self, j):
        return self.first_y + j.astype(jnp.float32) * SPACING

    def wz(self, half):
        return row_index().astype(jnp.float32) * SPACING + (FIRST + half * TILE * SPACING)

    def from_y(self, values):
        return pltpu.roll(values, self.shift_y, 1)

    def from_z(self, values, half):
        if half:
            return jnp.where(self.lane == 0, pltpu.roll(values, 128 + 1 - NZ, 1), pltpu.roll(values, 1, 1))
        return jnp.where(self.lane == NZ - 1, pltpu.roll(values, NZ - 1, 1), pltpu.roll(values, 127, 1))


def trace(low, middle, high, sign):
    return low + sign * middle + high


def trace_z(low, middle, high, half):
    return low + middle + high if half else low - middle + high


def one_direction(rates, coefs, index, upper, inflow, speed, size):
    _, i1, i2 = index
    jump = -upper if inflow is None else inflow - upper
    parts = (
        size * jump,
        (-3.0 * speed) * jump - (6.0 * size) * coefs[i1] - (6.0 * speed) * coefs[i2],
        (5.0 * size) * jump + (10.0 * speed) * coefs[i1],
    )
    for i, part in zip(index, parts):
        rates[i] = part if rates[i] is None else rates[i] + part


def transport(place, coefs, inflow_x, j, half):
    rates = [None] * 27
    for b in range(3):
        for c in range(3):
            index = [mode(a, b, c) for a in range(3)]
            upper = trace(*(coefs[i] for i in index), place.sx)
            one_direction(rates, coefs, index, upper, inflow_x and inflow_x[3 * b + c], place.wx, place.ax)
    wy = place.wy(j)
    ay = wy * place.sy
    for a in range(3):
        for c in range(3):
            index = [mode(a, b, c) for b in range(3)]
            upper = trace(*(coefs[i] for i in index), place.sy)
            one_direction(rates, coefs, index, upper, place.from_y(upper), wy, ay)
    wz = place.wz(half)
    az = wz if half else -wz
    for a in range(3):
        for b in range(3):
            index = [mode(a, b, c) for c in range(3)]
            upper = trace_z(*(coefs[i] for i in index), half)
            one_direction(rates, coefs, index, upper, place.from_z(upper, half), wz, az)
    return rates


def velocity_groups(body):
    def step(j, carry):
        for half in range(2):
            carry = body(j, half, pl.multiple_of((2 * j + half) * TILE, TILE), carry)
        return carry

    return step


def load_coefs(field, start):
    return [field[pl.ds(start * 27 + m, TILE, stride=27), :] for m in range(27)]


def moments(place, j, half, values):
    wy = place.wy(j)
    wz = place.wz(half)
    return [values, wy * values, wz * values, (0.5 * (wy * wy + wz * wz)) * values]


def all_moments(wx, four):
    total = lambda values: jnp.sum(values, axis=0, keepdims=True)
    count, along_y, along_z, energy = four
    return [
        total(count),
        total(wx * count),
        total(along_y),
        total(along_z),
        total(energy + (0.5 * (wx * wx)) * count),
    ]


def chunk_copy(source, target, sems, j):
    rows = pl.ds(pl.multiple_of(j * CHUNK, CHUNK), CHUNK)
    return pltpu.make_async_copy(source.at[rows], target.at[rows], sems.at[j])


def send_moments(place, field, column, column_hbm, sem):
    def sums_of(j, half, start, sums):
        base, x1, x2, y1, y2, z1, z2 = (
            field[pl.ds(start * 27 + m, TILE, stride=27), :] for m in (0, 9, 18, 3, 6, 1, 2)
        )
        out_x = place.ax * trace(base, x1, x2, place.sx)
        upper_y = trace(base, y1, y2, place.sy)
        upper_z = trace_z(base, z1, z2, half)
        wy = place.wy(j)
        wz = place.wz(half)
        kept = (wy * place.sy) * (place.from_y(upper_y) - upper_y) - out_x
        kept = kept + (wz if half else -wz) * (place.from_z(upper_z, half) - upper_z)
        terms = moments(place, j, half, base) + moments(place, j, half, kept) + moments(place, j, half, out_x)
        return tuple(s + t for s, t in zip(sums, terms))

    zero = jnp.zeros((TILE, 128), jnp.float32)
    sums = lax.fori_loop(0, 4, velocity_groups(sums_of), (zero,) * 12)
    for i, s in enumerate(sums):
        row = WEIGHT * jnp.sum(s, axis=0, keepdims=True)
        column[pl.ds(i, NZ, stride=COLUMN_ROWS), :] = jnp.broadcast_to(row, (NZ, 128))
    copy = pltpu.make_async_copy(column, column_hbm, sem)
    copy.start()
    copy.wait()


def first_kernel(field_hbm, rate_hbm, halo, column_hbm, field, rate, column, sems):
    place = Place()
    for j in range(4):
        chunk_copy(field_hbm, field, sems, j).start()
    rate_copy = pltpu.make_async_copy(rate_hbm, rate, sems.at[4])
    rate_copy.start()

    def traces_of(j, half, start, carry):
        if not half:
            chunk_copy(field_hbm, field, sems, j).wait()
        coefs = load_coefs(field, start)
        for k in range(9):
            halo[pl.ds(k * COUNT + start, TILE), :] = trace(coefs[k], coefs[9 + k], coefs[18 + k], place.sx)
        return carry

    lax.fori_loop(0, 4, velocity_groups(traces_of), 0)
    rate_copy.wait()

    @pl.when(place.waits)
    def _():
        send_moments(place, field, column, column_hbm, sems.at[5])


def moments_kernel(field, _, column_hbm, column, sems):
    place = Place()

    @pl.when(jnp.logical_not(place.waits))
    def _():
        send_moments(place, field, column, column_hbm, sems.at[0])


def between_kernel(column, planes):
    place = Place()
    source = lax.broadcasted_iota(jnp.int32, (NZ, 128), 0)
    source = (source + LEAD) % NZ // 2 + place.vel // (VELS // 2) * (VPD // 2)
    wx = source.astype(jnp.float32) * SPACING + FIRST
    rows = [column[pl.ds(i, NZ, stride=COLUMN_ROWS), :] for i in range(COLUMN_ROWS)]
    held, kept, gone = (all_moments(wx, rows[k : k + 4]) for k in (0, 4, 8))
    for i in range(5):
        planes[pl.ds(i, 4 * BOXES, stride=PLANE_ROWS), :] = jnp.broadcast_to(held[i], (4 * BOXES, 128))
        box = (lax.broadcasted_iota(jnp.int32, (4 * BOXES, 128), 0) + PLANE_LEAD) % BOXES
        sent = jnp.where(box == place.box, kept[i], jnp.where(box == place.downwind, gone[i], 0.0))
        planes[pl.ds(5 + i, 4 * BOXES, stride=PLANE_ROWS), :] = sent


def second_kernel(field, rate, halo, middle, halo_out):
    place = Place()
    collision = jnp.broadcast_to(rate[...], (TILE, 128))

    def body(j, half, start, carry):
        coefs = load_coefs(field, start)
        inflow = [halo[pl.ds(k * COUNT + start, TILE), :] for k in range(9)]
        rates = transport(place, coefs, inflow, j, half)
        new = [c + STEP * (r - collision * c) for c, r in zip(coefs, rates)]
        for m in range(27):
            middle[pl.ds(m * COUNT + start, TILE), :] = new[m]
        for k in range(9):
            halo_out[pl.ds(k * COUNT + start, TILE), :] = trace(new[k], new[9 + k], new[18 + k], place.sx)
        return carry

    lax.fori_loop(0, 4, velocity_groups(body), 0)
    halo_out[FACE - TILE :, :] = collision


def base_kernel(field, rate, middle, base):
    place = Place()
    collision = jnp.broadcast_to(rate[...], (TILE, 128))

    def body(j, half, start, carry):
        coefs = [middle[pl.ds(m * COUNT + start, TILE), :] for m in range(27)]
        rates = transport(place, coefs, None, j, half)
        for m in range(27):
            moved = coefs[m] + STEP * (rates[m] - collision * coefs[m])
            old = field[pl.ds(start * 27 + m, TILE, stride=27), :]
            base[pl.ds(m * COUNT + start, TILE), :] = 0.5 * old + 0.5 * moved
        return carry

    lax.fori_loop(0, 4, velocity_groups(body), 0)


def states(totals):
    density = totals[0]
    flow = [t / density for t in totals[1:4]]
    square = flow[0] * flow[0] + flow[1] * flow[1] + flow[2] * flow[2]
    temper = (2.0 * totals[4] / density - square) / 3.0
    spread = 2.0 * math.pi * temper
    return flow, density / (spread * jnp.sqrt(spread)), 0.5 / temper


def maxwell_moments(state):
    flow, scale, inverse = state
    centres = lax.broadcasted_iota(jnp.int32, (16, 128), 0).astype(jnp.float32) * SPACING + FIRST
    sums = []
    for u in flow:
        offset = centres - u
        bell = jnp.exp(-(offset * offset) * inverse)
        sums.append([jnp.sum(v, axis=0, keepdims=True) for v in (bell, centres * bell, centres * centres * bell)])
    (x0, x1, x2), (y0, y1, y2), (z0, z1, z2) = sums
    scale = WEIGHT * scale
    energy = x2 * y0 * z0 + x0 * y2 * z0 + x0 * y0 * z2
    return [
        scale * (x0 * y0 * z0),
        scale * (x1 * y0 * z0),
        scale * (x0 * y1 * z0),
        scale * (x0 * y0 * z1),
        scale * (0.5 * energy),
    ]


def third_kernel(rate, halo, planes, base, out_hbm, out, sems):
    place = Place()

    box = (lax.broadcasted_iota(jnp.int32, (4 * BOXES, 128), 0) + PLANE_LEAD) % BOXES
    rows = [planes[pl.ds(i, 4 * BOXES, stride=PLANE_ROWS), :] for i in range(PLANE_ROWS)]
    total = lambda values: jnp.sum(values, axis=0, keepdims=True)
    totals = [total(jnp.where(box == place.box, r, 0.0)) for r in rows[:5]]
    upwind = [total(jnp.where(box == place.upwind, r, 0.0)) for r in rows[:5]]
    flux = [total(r) for r in rows[5:]]
    nu = rate[...]
    upwind_nu = halo[FACE - 1 :, :]
    now = states(totals)
    gains = maxwell_moments(now)
    later = states([t + STEP * (f - nu * t + nu * g) for t, f, g in zip(totals, flux, gains)])
    before = states(upwind)

    def spread_out(state, factor):
        flow, scale, inverse = state
        wide = lambda v: jnp.broadcast_to(v, (TILE, 128))
        part = (place.wx - flow[0]) * (place.wx - flow[0])
        return wide(part), wide(flow[1]), wide(flow[2]), wide(factor * scale), wide(-inverse)

    now = spread_out(now, STEP * nu)
    before = spread_out(before, STEP * upwind_nu)
    later = spread_out(later, HALF_STEP * nu)
    gain = HALF_STEP * place.ax
    speed = HALF_STEP * place.wx
    collision = jnp.broadcast_to(nu, (TILE, 128))

    def body(j, half, start, carry):
        wy = place.wy(j)
        wz = place.wz(half)

        def bell(state):
            part, flow_y, flow_z, scale, inverse = state
            off_y = wy - flow_y
            off_z = wz - flow_z
            return scale * jnp.exp((part + off_y * off_y + off_z * off_z) * inverse)

        added = [None] * 27
        extra = bell(now)
        inflow = [halo[pl.ds(k * COUNT + start, TILE), :] for k in range(9)]
        inflow[0] = inflow[0] + bell(before) - extra
        for k in range(9):
            added[k] = gain * inflow[k]
            added[9 + k] = (-3.0 * speed) * inflow[k]
            added[18 + k] = (5.0 * gain) * inflow[k]
        added[0] = added[0] + (0.5 - HALF_STEP * collision) * extra + bell(later)
        lines = (
            (HALF_STEP * wy, HALF_STEP * (wy * place.sy), place.from_y(extra) - extra, 3),
            (HALF_STEP * wz, HALF_STEP * (wz if half else -wz), place.from_z(extra, half) - extra, 1),
        )
        for line, size, jump, i in lines:
            added[0] = added[0] + size * jump
            added[i] = added[i] - (3.0 * line) * jump
            added[2 * i] = added[2 * i] + (5.0 * size) * jump
        for m in range(27):
            out[pl.ds(start * 27 + m, TILE, stride=27), :] = base[pl.ds(m * COUNT + start, TILE), :] + added[m]
        if half:
            chunk_copy(out, out_hbm, sems, j).start()
        return carry

    lax.fori_loop(0, 4, velocity_groups(body), 0)
    for j in range(4):
        chunk_copy(out, out_hbm, sems, j).wait()


def call(kernel, outs, *args, remote_in=(), remote_out=(), scratch=(), aliases=None):
    vmem = pl.BlockSpec(memory_space=pltpu.VMEM)
    hbm = pl.BlockSpec(memory_space=pltpu.HBM)
    shapes = [jax.ShapeDtypeStruct(s, jnp.float32) for s in outs]
    moved = sum(4 * math.prod(s) for s in outs) + sum(4 * a.size for a in args)
    return pl.pallas_call(
        kernel,
        out_shape=shapes,
        in_specs=[hbm if i in remote_in else vmem for i in range(len(args))],
        out_specs=[hbm if i in remote_out else vmem for i in range(len(outs))],
        scratch_shapes=scratch,
        input_output_aliases=aliases or {},
        compiler_params=pltpu.CompilerParams(vmem_limit_bytes=GRANT),
        cost_estimate=pl.CostEstimate(flops=4000000, bytes_accessed=moved, transcendentals=30000),
    )(*args)


def downwind_pairs():
    pairs = []
    for vel in range(VELS):
        step = 1 if vel >= VELS // 2 else BOXES - 1
        for box in range(BOXES):
            pairs.append((vel * BOXES + box, vel * BOXES + (box + step) % BOXES))
    return pairs


def vel_of(x, z, core):
    return x * 32 + z * 2 + core


PLANES = [
    [vel_of(x, z, core) * BOXES + box for x in range(2) for core in range(2) for box in range(BOXES)]
    for z in range(NZ)
]
PLANES = [group[PLANE_LEAD:] + group[:PLANE_LEAD] for group in PLANES]
COLUMNS = [[vel_of(x, (z + LEAD) % NZ, core) for z in range(NZ)] for x in range(2) for core in range(2)]


def exchange(blocks, axis, groups):
    count = len(groups[0])
    moved = lax.all_to_all(blocks.reshape(count, 1, -1), axis, 0, 0, axis_index_groups=groups)
    return moved.reshape(blocks.shape)


def step(distribution, collision_rate):
    field = pltpu.with_memory_space_constraint(distribution.reshape(COUNT * 27, 128), pltpu.HBM)
    collision_rate = pltpu.with_memory_space_constraint(collision_rate, pltpu.HBM)
    face = (9 * COUNT, 128)
    marked = (FACE, 128)
    whole = (27 * COUNT, 128)
    halo, column, field, rate = call(
        first_kernel,
        [face, (NZ * COLUMN_ROWS, 128), whole, (1, 128)],
        field,
        collision_rate,
        remote_in=(0, 1),
        remote_out=(1,),
        scratch=[pltpu.VMEM((NZ * COLUMN_ROWS, 128), jnp.float32), pltpu.SemaphoreType.DMA((6,))],
    )
    halo = lax.ppermute(halo, ("vel", "box"), downwind_pairs())
    (column,) = call(
        moments_kernel,
        [(NZ * COLUMN_ROWS, 128)],
        field,
        column,
        remote_in=(1,),
        remote_out=(0,),
        scratch=[pltpu.VMEM((NZ * COLUMN_ROWS, 128), jnp.float32), pltpu.SemaphoreType.DMA((1,))],
        aliases={1: 0},
    )
    column = exchange(column, "vel", COLUMNS)
    middle, halo = call(second_kernel, [whole, marked], field, rate, halo)
    halo = lax.ppermute(halo, ("vel", "box"), downwind_pairs())
    (base,) = call(base_kernel, [whole], field, rate, middle)
    (planes,) = call(between_kernel, [(4 * BOXES * PLANE_ROWS, 128)], column)
    planes = exchange(planes, ("vel", "box"), PLANES)
    (out,) = call(
        third_kernel,
        [whole],
        rate,
        halo,
        planes,
        base,
        remote_out=(0,),
        scratch=[pltpu.VMEM(whole, jnp.float32), pltpu.SemaphoreType.DMA((4,))],
    )
    return out.reshape(distribution.shape)


def solution(mesh):
    return jax.shard_map(
        step,
        mesh=mesh,
        in_specs=(P("vel", None, None, None, "box", None), P("box", None)),
        out_specs=P("vel", None, None, None, "box", None),
        check_vma=False,
    )
```

```python
import math

import jax
import jax.numpy as jnp
from jax import lax
from jax.experimental import pallas as pl
from jax.experimental.pallas import tpu as pltpu
from jax.sharding import PartitionSpec as P


NZ = 16
VPD = 16
VELS = 64
LEAD = 10
PLANE_LEAD = 14
BOXES = 8
COUNT = 64
STEP = 0.02
HALF_STEP = 0.5 * STEP
SPACING = 0.5
FIRST = -3.75
WEIGHT = SPACING**3
COLUMN_ROWS = 12
PLANE_ROWS = 10
TILE = 8
GRANT = 16 << 20
CHUNK = COUNT * 27 // 4
FACE = 9 * COUNT + TILE


def mode(a, b, c):
    return 9 * a + 3 * b + c


def row_index():
    return lax.broadcasted_iota(jnp.int32, (TILE, 128), 0)


class Place:
    def __init__(self):
        self.vel = lax.axis_index("vel")
        self.box = lax.axis_index("box")
        right = self.vel >= VELS // 2
        self.sx = jnp.where(right, 1.0, -1.0)
        self.wx = (self.vel // 4).astype(jnp.float32) * SPACING + FIRST
        self.ax = self.wx * self.sx
        up = self.vel % 4 >= 2
        self.sy = jnp.where(up, 1.0, -1.0)
        self.first_y = (self.vel % 4 * 4).astype(jnp.float32) * SPACING + FIRST
        self.shift_y = jnp.where(up, NZ, 128 - NZ)
        self.upwind = jnp.where(right, (self.box + BOXES - 1) % BOXES, (self.box + 1) % BOXES)
        self.downwind = jnp.where(right, (self.box + 1) % BOXES, (self.box + BOXES - 1) % BOXES)
        self.waits = jnp.logical_not(right) & (self.box % (BOXES // 2) == 0)
        self.lane = lax.broadcasted_iota(jnp.int32, (TILE, 128), 1) % NZ

    def wy(self, j):
        return self.first_y + j.astype(jnp.float32) * SPACING

    def wz(self, half):
        return row_index().astype(jnp.float32) * SPACING + (FIRST + half * TILE * SPACING)

    def from_y(self, values):
        return pltpu.roll(values, self.shift_y, 1)

    def from_z(self, values, half):
        if half:
            return jnp.where(self.lane == 0, pltpu.roll(values, 128 + 1 - NZ, 1), pltpu.roll(values, 1, 1))
        return jnp.where(self.lane == NZ - 1, pltpu.roll(values, NZ - 1, 1), pltpu.roll(values, 127, 1))


def trace(low, middle, high, sign):
    return low + sign * middle + high


def trace_z(low, middle, high, half):
    return low + middle + high if half else low - middle + high


def one_direction(rates, coefs, index, upper, inflow, speed, size):
    _, i1, i2 = index
    jump = -upper if inflow is None else inflow - upper
    parts = (
        size * jump,
        (-3.0 * speed) * jump - (6.0 * size) * coefs[i1] - (6.0 * speed) * coefs[i2],
        (5.0 * size) * jump + (10.0 * speed) * coefs[i1],
    )
    for i, part in zip(index, parts):
        rates[i] = part if rates[i] is None else rates[i] + part


def transport(place, coefs, inflow_x, j, half):
    rates = [None] * 27
    for b in range(3):
        for c in range(3):
            index = [mode(a, b, c) for a in range(3)]
            upper = trace(*(coefs[i] for i in index), place.sx)
            one_direction(rates, coefs, index, upper, inflow_x and inflow_x[3 * b + c], place.wx, place.ax)
    wy = place.wy(j)
    ay = wy * place.sy
    for a in range(3):
        for c in range(3):
            index = [mode(a, b, c) for b in range(3)]
            upper = trace(*(coefs[i] for i in index), place.sy)
            one_direction(rates, coefs, index, upper, place.from_y(upper), wy, ay)
    wz = place.wz(half)
    az = wz if half else -wz
    for a in range(3):
        for b in range(3):
            index = [mode(a, b, c) for c in range(3)]
            upper = trace_z(*(coefs[i] for i in index), half)
            one_direction(rates, coefs, index, upper, place.from_z(upper, half), wz, az)
    return rates


def velocity_groups(body):
    def step(j, carry):
        for half in range(2):
            carry = body(j, half, pl.multiple_of((2 * j + half) * TILE, TILE), carry)
        return carry

    return step


def load_coefs(field, start):
    return [field[pl.ds(start * 27 + m, TILE, stride=27), :] for m in range(27)]


def moments(place, j, half, values):
    wy = place.wy(j)
    wz = place.wz(half)
    return [values, wy * values, wz * values, (0.5 * (wy * wy + wz * wz)) * values]


def all_moments(wx, four):
    total = lambda values: jnp.sum(values, axis=0, keepdims=True)
    count, along_y, along_z, energy = four
    return [
        total(count),
        total(wx * count),
        total(along_y),
        total(along_z),
        total(energy + (0.5 * (wx * wx)) * count),
    ]


def chunk_copy(source, target, sems, j, size=CHUNK):
    rows = pl.ds(pl.multiple_of(j * size, size), size)
    return pltpu.make_async_copy(source.at[rows], target.at[rows], sems.at[j])


def send_moments(place, field, column, column_hbm, sem):
    def sums_of(j, half, start, sums):
        base, x1, x2, y1, y2, z1, z2 = (
            field[pl.ds(start * 27 + m, TILE, stride=27), :] for m in (0, 9, 18, 3, 6, 1, 2)
        )
        out_x = place.ax * trace(base, x1, x2, place.sx)
        upper_y = trace(base, y1, y2, place.sy)
        upper_z = trace_z(base, z1, z2, half)
        wy = place.wy(j)
        wz = place.wz(half)
        kept = (wy * place.sy) * (place.from_y(upper_y) - upper_y) - out_x
        kept = kept + (wz if half else -wz) * (place.from_z(upper_z, half) - upper_z)
        terms = moments(place, j, half, base) + moments(place, j, half, kept) + moments(place, j, half, out_x)
        return tuple(s + t for s, t in zip(sums, terms))

    zero = jnp.zeros((TILE, 128), jnp.float32)
    sums = lax.fori_loop(0, 4, velocity_groups(sums_of), (zero,) * 12)
    for i, s in enumerate(sums):
        row = WEIGHT * jnp.sum(s, axis=0, keepdims=True)
        column[pl.ds(i, NZ, stride=COLUMN_ROWS), :] = jnp.broadcast_to(row, (NZ, 128))
    copy = pltpu.make_async_copy(column, column_hbm, sem)
    copy.start()
    copy.wait()


def first_kernel(field_hbm, rate_hbm, halo, column_hbm, field, rate, column, sems):
    place = Place()
    for j in range(4):
        chunk_copy(field_hbm, field, sems, j).start()
    rate_copy = pltpu.make_async_copy(rate_hbm, rate, sems.at[4])
    rate_copy.start()

    def traces_of(j, half, start, carry):
        if not half:
            chunk_copy(field_hbm, field, sems, j).wait()
        coefs = load_coefs(field, start)
        for k in range(9):
            halo[pl.ds(k * COUNT + start, TILE), :] = trace(coefs[k], coefs[9 + k], coefs[18 + k], place.sx)
        return carry

    lax.fori_loop(0, 4, velocity_groups(traces_of), 0)
    rate_copy.wait()

    @pl.when(place.waits)
    def _():
        send_moments(place, field, column, column_hbm, sems.at[5])


def moments_kernel(field, _, column_hbm, column, sems):
    place = Place()

    @pl.when(jnp.logical_not(place.waits))
    def _():
        send_moments(place, field, column, column_hbm, sems.at[0])


def between_kernel(column, planes):
    place = Place()
    source = lax.broadcasted_iota(jnp.int32, (NZ, 128), 0)
    source = (source + LEAD) % NZ // 2 + place.vel // (VELS // 2) * (VPD // 2)
    wx = source.astype(jnp.float32) * SPACING + FIRST
    rows = [column[pl.ds(i, NZ, stride=COLUMN_ROWS), :] for i in range(COLUMN_ROWS)]
    held, kept, gone = (all_moments(wx, rows[k : k + 4]) for k in (0, 4, 8))
    for i in range(5):
        planes[pl.ds(i, 4 * BOXES, stride=PLANE_ROWS), :] = jnp.broadcast_to(held[i], (4 * BOXES, 128))
        box = (lax.broadcasted_iota(jnp.int32, (4 * BOXES, 128), 0) + PLANE_LEAD) % BOXES
        sent = jnp.where(box == place.box, kept[i], jnp.where(box == place.downwind, gone[i], 0.0))
        planes[pl.ds(5 + i, 4 * BOXES, stride=PLANE_ROWS), :] = sent


def second_kernel(field, rate, halo, middle, halo_out):
    place = Place()
    collision = jnp.broadcast_to(rate[...], (TILE, 128))

    def body(j, half, start, carry):
        coefs = load_coefs(field, start)
        inflow = [halo[pl.ds(k * COUNT + start, TILE), :] for k in range(9)]
        rates = transport(place, coefs, inflow, j, half)
        new = [c + STEP * (r - collision * c) for c, r in zip(coefs, rates)]
        for m in range(27):
            middle[pl.ds(m * COUNT + start, TILE), :] = new[m]
        for k in range(9):
            halo_out[pl.ds(k * COUNT + start, TILE), :] = trace(new[k], new[9 + k], new[18 + k], place.sx)
        return carry

    lax.fori_loop(0, 4, velocity_groups(body), 0)
    halo_out[FACE - TILE :, :] = collision


def base_kernel(field, rate, middle, base):
    place = Place()
    collision = jnp.broadcast_to(rate[...], (TILE, 128))

    def body(j, half, start, carry):
        coefs = [middle[pl.ds(m * COUNT + start, TILE), :] for m in range(27)]
        rates = transport(place, coefs, None, j, half)
        for m in range(27):
            moved = coefs[m] + STEP * (rates[m] - collision * coefs[m])
            old = field[pl.ds(start * 27 + m, TILE, stride=27), :]
            base[pl.ds(m * COUNT + start, TILE), :] = 0.5 * old + 0.5 * moved
        return carry

    lax.fori_loop(0, 4, velocity_groups(body), 0)


def states(totals):
    density = totals[0]
    inverse = 1.0 / density
    flow = [t * inverse for t in totals[1:4]]
    square = flow[0] * flow[0] + flow[1] * flow[1] + flow[2] * flow[2]
    temper = (2.0 * totals[4] * inverse - square) * (1.0 / 3.0)
    spread = 2.0 * math.pi * temper
    return flow, density / (spread * jnp.sqrt(spread)), 0.5 / temper


def maxwell_moments(state):
    flow, scale, inverse = state
    centres = lax.broadcasted_iota(jnp.int32, (16, 128), 0).astype(jnp.float32) * SPACING + FIRST
    sums = []
    for u in flow:
        offset = centres - u
        bell = jnp.exp(-(offset * offset) * inverse)
        sums.append([jnp.sum(v, axis=0, keepdims=True) for v in (bell, centres * bell, centres * centres * bell)])
    (x0, x1, x2), (y0, y1, y2), (z0, z1, z2) = sums
    scale = WEIGHT * scale
    energy = x2 * y0 * z0 + x0 * y2 * z0 + x0 * y0 * z2
    return [
        scale * (x0 * y0 * z0),
        scale * (x1 * y0 * z0),
        scale * (x0 * y1 * z0),
        scale * (x0 * y0 * z1),
        scale * (0.5 * energy),
    ]


def third_kernel(rate, halo, planes, base, out_hbm, out, sems):
    place = Place()

    box = (lax.broadcasted_iota(jnp.int32, (4 * BOXES, 128), 0) + PLANE_LEAD) % BOXES
    rows = [planes[pl.ds(i, 4 * BOXES, stride=PLANE_ROWS), :] for i in range(PLANE_ROWS)]
    total = lambda values: jnp.sum(values, axis=0, keepdims=True)
    totals = [total(jnp.where(box == place.box, r, 0.0)) for r in rows[:5]]
    upwind = [total(jnp.where(box == place.upwind, r, 0.0)) for r in rows[:5]]
    flux = [total(r) for r in rows[5:]]
    nu = rate[...]
    upwind_nu = halo[FACE - 1 :, :]
    now = states(totals)
    gains = maxwell_moments(now)
    later = states([t + STEP * (f - nu * t + nu * g) for t, f, g in zip(totals, flux, gains)])
    before = states(upwind)

    def spread_out(state, factor):
        flow, scale, inverse = state
        wide = lambda v: jnp.broadcast_to(v, (TILE, 128))
        part = (place.wx - flow[0]) * (place.wx - flow[0])
        return wide(part), wide(flow[1]), wide(flow[2]), wide(factor * scale), wide(-inverse)

    now = spread_out(now, STEP * nu)
    before = spread_out(before, STEP * upwind_nu)
    later = spread_out(later, HALF_STEP * nu)
    gain = HALF_STEP * place.ax
    speed = HALF_STEP * place.wx
    collision = jnp.broadcast_to(nu, (TILE, 128))

    def body(j, half, start, carry):
        wy = place.wy(j)
        wz = place.wz(half)

        def bell(state):
            part, flow_y, flow_z, scale, inverse = state
            off_y = wy - flow_y
            off_z = wz - flow_z
            return scale * jnp.exp((part + off_y * off_y + off_z * off_z) * inverse)

        added = [None] * 27
        extra = bell(now)
        inflow = [halo[pl.ds(k * COUNT + start, TILE), :] for k in range(9)]
        inflow[0] = inflow[0] + bell(before) - extra
        for k in range(9):
            added[k] = gain * inflow[k]
            added[9 + k] = (-3.0 * speed) * inflow[k]
            added[18 + k] = (5.0 * gain) * inflow[k]
        added[0] = added[0] + (0.5 - HALF_STEP * collision) * extra + bell(later)
        lines = (
            (HALF_STEP * wy, HALF_STEP * (wy * place.sy), place.from_y(extra) - extra, 3),
            (HALF_STEP * wz, HALF_STEP * (wz if half else -wz), place.from_z(extra, half) - extra, 1),
        )
        for line, size, jump, i in lines:
            added[0] = added[0] + size * jump
            added[i] = added[i] - (3.0 * line) * jump
            added[2 * i] = added[2 * i] + (5.0 * size) * jump
        for m in range(27):
            out[pl.ds(start * 27 + m, TILE, stride=27), :] = base[pl.ds(m * COUNT + start, TILE), :] + added[m]
        chunk_copy(out, out_hbm, sems, 2 * j + half, CHUNK // 2).start()
        return carry

    lax.fori_loop(0, 4, velocity_groups(body), 0)
    for j in range(8):
        chunk_copy(out, out_hbm, sems, j, CHUNK // 2).wait()


def call(kernel, outs, *args, remote_in=(), remote_out=(), scratch=(), aliases=None):
    vmem = pl.BlockSpec(memory_space=pltpu.VMEM)
    hbm = pl.BlockSpec(memory_space=pltpu.HBM)
    shapes = [jax.ShapeDtypeStruct(s, jnp.float32) for s in outs]
    moved = sum(4 * math.prod(s) for s in outs) + sum(4 * a.size for a in args)
    return pl.pallas_call(
        kernel,
        out_shape=shapes,
        in_specs=[hbm if i in remote_in else vmem for i in range(len(args))],
        out_specs=[hbm if i in remote_out else vmem for i in range(len(outs))],
        scratch_shapes=scratch,
        input_output_aliases=aliases or {},
        compiler_params=pltpu.CompilerParams(vmem_limit_bytes=GRANT),
        cost_estimate=pl.CostEstimate(flops=4000000, bytes_accessed=moved, transcendentals=30000),
    )(*args)


def downwind_pairs():
    pairs = []
    for vel in range(VELS):
        step = 1 if vel >= VELS // 2 else BOXES - 1
        for box in range(BOXES):
            pairs.append((vel * BOXES + box, vel * BOXES + (box + step) % BOXES))
    return pairs


def vel_of(x, z, core):
    return x * 32 + z * 2 + core


PLANES = [
    [vel_of(x, z, core) * BOXES + box for x in range(2) for core in range(2) for box in range(BOXES)]
    for z in range(NZ)
]
PLANES = [group[PLANE_LEAD:] + group[:PLANE_LEAD] for group in PLANES]
COLUMNS = [[vel_of(x, (z + LEAD) % NZ, core) for z in range(NZ)] for x in range(2) for core in range(2)]


def exchange(blocks, axis, groups):
    count = len(groups[0])
    moved = lax.all_to_all(blocks.reshape(count, 1, -1), axis, 0, 0, axis_index_groups=groups)
    return moved.reshape(blocks.shape)


def step(distribution, collision_rate):
    field = pltpu.with_memory_space_constraint(distribution.reshape(COUNT * 27, 128), pltpu.HBM)
    collision_rate = pltpu.with_memory_space_constraint(collision_rate, pltpu.HBM)
    face = (9 * COUNT, 128)
    marked = (FACE, 128)
    whole = (27 * COUNT, 128)
    halo, column, field, rate = call(
        first_kernel,
        [face, (NZ * COLUMN_ROWS, 128), whole, (1, 128)],
        field,
        collision_rate,
        remote_in=(0, 1),
        remote_out=(1,),
        scratch=[pltpu.VMEM((NZ * COLUMN_ROWS, 128), jnp.float32), pltpu.SemaphoreType.DMA((6,))],
    )
    halo = lax.ppermute(halo, ("vel", "box"), downwind_pairs())
    (column,) = call(
        moments_kernel,
        [(NZ * COLUMN_ROWS, 128)],
        field,
        column,
        remote_in=(1,),
        remote_out=(0,),
        scratch=[pltpu.VMEM((NZ * COLUMN_ROWS, 128), jnp.float32), pltpu.SemaphoreType.DMA((1,))],
        aliases={1: 0},
    )
    column = exchange(column, "vel", COLUMNS)
    middle, halo = call(second_kernel, [whole, marked], field, rate, halo)
    halo = lax.ppermute(halo, ("vel", "box"), downwind_pairs())
    (base,) = call(base_kernel, [whole], field, rate, middle)
    (planes,) = call(between_kernel, [(4 * BOXES * PLANE_ROWS, 128)], column)
    planes = exchange(planes, ("vel", "box"), PLANES)
    (out,) = call(
        third_kernel,
        [whole],
        rate,
        halo,
        planes,
        base,
        remote_out=(0,),
        scratch=[pltpu.VMEM(whole, jnp.float32), pltpu.SemaphoreType.DMA((8,))],
    )
    return out.reshape(distribution.shape)


def solution(mesh):
    return jax.shard_map(
        step,
        mesh=mesh,
        in_specs=(P("vel", None, None, None, "box", None), P("box", None)),
        out_specs=P("vel", None, None, None, "box", None),
        check_vma=False,
    )
```
